32 devices in a mesh: grp: 4 (over y, core), row: 8 (over z, x).
Axes of the slice: x: 2, y: 2, z: 4, core: 2. Of those that a mesh axis runs over, the one named last changes fastest.
Arguments:
- grad: float32 [32, 2048, 512], P('grp', 'row')
- weight: bfloat16 [32, 2048, 512], P('grp', 'row'), may hold values from -0.125 to 0.125
- owner: int32 [32, 1], P('grp'), may hold values from 0 to 7; in each aligned block of 8 rows (0 to 7, 8 to 15, ...) at most 2 rows name the same one
- tokens: bfloat16 [3072, 2048], P('row'), may hold values from -6 to 6
- counts: int32 [8], P('row'), may hold values from 96 to 384, as said below
Outputs:
- new_weight: bfloat16 [32, 2048, 512], P('grp', 'row')
- mixed: bfloat16 [3072, 512], P('row', 'grp')
The draws below stay inside these ranges and needn't reach their ends.
Inputs may be any that keep to these rules, and one draw needn't show every extreme that they name: Within each group's 8 consecutive matrices no owner is named more than 2 times, a bound that some block reaches. `counts`: some row index has all 384 rows live.
All inputs are finite; a program needn't handle non-finite values.
Results may differ from the reference program's by a relative error of at most 0.017.
Values may be sent and summed in bfloat16 or wider, within the bound.
A program may use at most 128 MiB of HBM per device.

```python
import math
import jax
import jax.numpy as jnp
import numpy as np
from jax import lax

H = 2048
F = 512
TOK_DEV = 384
ITERS = 5
MOST = 2
EXP_G = 8
EXPERTS = 32
TOKENS = 3072
N_GRP = 4
N_ROW = 8


def draw_grad(key, part):
    keys = jax.random.split(jax.random.fold_in(key, 11), 3)
    shape = (EXPERTS, H, F)
    base = jax.random.normal(keys[0], shape, jnp.float32)
    row_scale = jnp.exp(jax.random.uniform(keys[1], (EXPERTS, H, 1), jnp.float32) * math.log(10.0))
    rising = jnp.exp(math.log(3.0) * jnp.arange(H, dtype=jnp.float32) / H)[None, :, None]
    col_scale = jnp.exp(jax.random.uniform(keys[2], (EXPERTS, 1, F), jnp.float32) * math.log(10.0))
    return base * row_scale * rising * col_scale


def draw_counts(key, part):
    keys = jax.random.split(jax.random.fold_in(key, 23), 2)
    values = jax.random.randint(keys[0], (N_ROW,), TOK_DEV // 4, TOK_DEV + 1)
    chosen = jax.random.randint(keys[1], (), 0, N_ROW)
    return jnp.where(jnp.arange(N_ROW) == chosen, TOK_DEV, values).astype(jnp.int32)


def block_scale(rng, dims, shards, least, largest):
    gain, own = 1.0, jax.random.fold_in(rng, 6)
    for position, shards_of in shards:
        steps = jnp.exp(jax.random.uniform(jax.random.fold_in(own, position), (shards_of,), jnp.float32, least / len(shards), largest / len(shards)))
        gain = gain * jnp.repeat(steps, dims[position] // shards_of).reshape([-1 if axis == position else 1 for axis in range(len(dims))])
    return gain


def routed_block(rng, own, number, rows, number_of, top, bound, slope):
    order = jax.random.permutation(rng, number_of)
    crowded, usual = portions_of(number_of, rows * top, bound, slope, True), portions_of(number_of, rows * top, bound, slope, False)
    places = jnp.arange(number_of)

    def named(sizes, turn):
        used = int((sizes > 0).sum())
        fixed = max(1, used // 4)
        passed = fixed + (places - fixed + turn * (used - fixed)) % max(1, number_of - fixed)
        return jnp.zeros((number_of,), jnp.int32).at[order[jnp.where(places < fixed, places, passed)]].set(jnp.asarray(sizes, jnp.int32))

    sizes = jnp.where(number % 4 == 0, named(crowded, number // 4), named(usual, number - number // 4 - 1))
    mixed = jax.random.permutation(jax.random.fold_in(own, 3), number_of)
    giver, sink = mixed[0:number_of // 2 * 2:2], mixed[1:number_of // 2 * 2:2]
    slack = jnp.minimum(sizes[giver] - 1, bound - sizes[sink]) // 2
    slack = jnp.where((giver == order[0]) | (sink == order[0]) | (sizes[sink] == 0), 0, jnp.maximum(slack, 0))
    passed = jax.random.randint(jax.random.fold_in(own, 4), (number_of // 2,), 0, 1 << 20) % (slack + 1)
    sizes = sizes.at[giver].add(-passed).at[sink].add(passed)
    labels = jnp.searchsorted(jnp.cumsum(sizes), jnp.arange(rows * top), side="right").astype(jnp.int32)
    grid = labels.reshape(top, rows).T
    grid = grid[jax.random.permutation(jax.random.fold_in(own, 1), rows)]
    turn = jax.random.randint(jax.random.fold_in(own, 2), (rows, 1), 0, top)
    return jnp.take_along_axis(grid, (jnp.arange(top)[None, :] + turn) % top, axis=1)


def portions_of(number_of, total, bound, slope, full):
    loads = [(1 << 20) // math.isqrt(grade ** slope) + 1 for grade in range(1, number_of + 1)]
    largest = bound if full else min(bound, max(-(-total // number_of), total * loads[0] // sum(loads)))
    least = 1 if total - largest >= number_of - 1 else 0
    given, spare = [largest] + [least] * (number_of - 1), total - largest - least * (number_of - 1)
    while spare > 0:
        free = [i for i in range(1, number_of) if given[i] < largest] or [i for i in range(1, number_of) if given[i] < bound]
        pool, left = sum([loads[i] for i in free]), spare
        for i in free:
            extra = min(bound - given[i], max(1, left * loads[i] // pool), spare)
            given[i] = given[i] + extra
            spare = spare - extra
    return np.array(given)


def gaussian(key, dims, spread, reach, shards=(), held_as=jnp.bfloat16):
    result = spread * jax.random.normal(key, dims, jnp.float32)
    if shards:
        result = result * block_scale(key, dims, shards, -0.22, 0.18)
    return jnp.clip(result, -reach, reach).astype(held_as)


def setup_inputs(seed: int = 0) -> dict:
    splits = jax.random.split(jax.random.key(seed), 6)
    grad = draw_grad(jax.random.fold_in(splits[5], 71), 0)
    weight = gaussian(splits[1], (EXPERTS, H, F), H ** -0.5, 0.125, ((0, 4), (1, 8)))
    owner_keys = jax.random.split(jax.random.fold_in(splits[2], 1), EXPERTS // EXP_G)
    owner_turns = jax.random.permutation(jax.random.fold_in(splits[2], 3), EXPERTS // EXP_G)
    owner = jax.vmap(lambda own, number: routed_block(jax.random.fold_in(splits[2], 2), own, number, EXP_G, N_ROW, 1, MOST, 2))(owner_keys, owner_turns).reshape((EXPERTS, 1))
    tokens = gaussian(splits[3], (TOKENS, H), 1.0, 6.0, ((0, 8),))
    counts = draw_counts(jax.random.fold_in(splits[5], 71), 0)
    return {"grad": grad, "weight": weight, "owner": owner, "tokens": tokens, "counts": counts}


coef_a = 3.4445
coef_b = -4.775
coef_c = 2.0315
step_size = 0.5

def newton_schulz(start):
    iterate_state = start
    for turn in range(ITERS):
        gram_product = jnp.dot(iterate_state.T, iterate_state, preferred_element_type=jnp.float32).astype(jnp.bfloat16)
        square = jnp.dot(gram_product, gram_product, preferred_element_type=jnp.float32)
        polynomial_term = (coef_b * gram_product.astype(jnp.float32) + coef_c * square).astype(jnp.bfloat16)
        iterate_state = (coef_a * iterate_state.astype(jnp.float32) + jnp.dot(iterate_state, polynomial_term, preferred_element_type=jnp.float32)).astype(jnp.bfloat16)
    return iterate_state

def reference(grad, weight, owner, tokens, counts):
    norm2 = lax.optimization_barrier(jnp.sum(grad * grad, axis=(1, 2)))
    start = (grad / (jnp.sqrt(norm2) + 1e-07)[:, None, None]).astype(jnp.bfloat16)
    blocks = tokens.reshape(N_ROW, TOK_DEV, H)

    def turn_one(total, item):
        matrix, old, target = item
        ortho = newton_schulz(matrix)
        recent_matrix = (old.astype(jnp.float32) - step_size * ortho.astype(jnp.float32)).astype(jnp.bfloat16)
        rows_in = lax.dynamic_index_in_dim(blocks, target, 0, keepdims=False)
        term = jnp.dot(rows_in, recent_matrix, preferred_element_type=jnp.float32)
        total = total.at[target].add(term)
        return (total, recent_matrix)
    initial_total0 = jnp.zeros((N_ROW, TOK_DEV, F), jnp.float32)
    total, new_weight = lax.scan(turn_one, initial_total0, (start, weight, owner[:, 0].astype(jnp.int32)))
    proj = total * N_GRP ** (-0.5)
    live = jnp.arange(TOK_DEV)[None, :, None] < counts[:, None, None]
    mixed = jnp.where(live, proj, 0.0).reshape(N_ROW * TOK_DEV, F).astype(jnp.bfloat16)
    return (new_weight, mixed)
```

```python
import functools

import jax
import jax.numpy as jnp
from jax import lax
from jax.experimental import pallas as pl
from jax.experimental.pallas import tpu as pltpu
from jax.sharding import PartitionSpec as P

ITERS = 5
MOST = 2
CORES = 2
LAGS = (1, 3)
TILE = 128

coef_a = 3.4445
coef_b = -4.775
coef_c = 2.0315
step_size = 0.5

f32 = jnp.float32
bf16 = jnp.bfloat16
MESH = pl.DeviceIdType.MESH


def far_first(n):
    return sorted(range(1, n), key=lambda k: abs(k - n // 2))


def greet(n, groups, grp_shifts):
    row, grp = lax.axis_index("row"), lax.axis_index("grp")
    barrier = pltpu.get_barrier_semaphore()
    for k in range(1, n):
        pl.semaphore_signal(
            barrier, inc=1, device_id=(grp, lax.rem(row + k, n)), device_id_type=MESH
        )
    for g in grp_shifts:
        pl.semaphore_signal(barrier, inc=1, device_id=(g, row), device_id_type=MESH)
    pl.semaphore_wait(barrier, n - 1 + len(grp_shifts))


def split(v):
    high = v.astype(bf16)
    return high, (v - high.astype(f32)).astype(bf16)


def dot(a, b):
    return jnp.dot(a, b, preferred_element_type=f32)


def dot_t(a, b):
    return lax.dot_general(a, b, (((0,), (0,)), ((), ())), preferred_element_type=f32)


def iotas(size):
    shape = (size, size)
    return lax.broadcasted_iota(jnp.int32, shape, 0), lax.broadcasted_iota(jnp.int32, shape, 1)


def block(i):
    return slice(i * TILE, (i + 1) * TILE)


def packed_rows(width):
    count = width // TILE
    return (count * (count - 1) // 2 + count // 2) * TILE + count // 2 * 8


def pack(full, out):
    count = full.shape[0] // TILE
    row, col = iotas(TILE)
    at = 0
    for i in range(count):
        for j in range(i + 1, count):
            out[at : at + TILE] = full[block(i), block(j)]
            at += TILE
    for i in range(0, count, 2):
        one, two = full[block(i), block(i)], full[block(i + 1), block(i + 1)]
        out[at : at + TILE] = jnp.where(row <= col, one, two)
        at += TILE
        diagonal = jnp.sum(jnp.where(row == col, two, 0.0), axis=0, keepdims=True)
        out[at : at + 8] = jnp.broadcast_to(diagonal, (8, TILE))
        at += 8


def unpack(packed, put):
    count = 1
    while packed_rows(count * TILE) < packed.shape[0]:
        count += 1
    row, col = iotas(TILE)
    at = 0
    for i in range(count):
        for j in range(i + 1, count):
            value = packed[at : at + TILE]
            put(i, j, value)
            put(j, i, value.T)
            at += TILE
    for i in range(0, count, 2):
        both = packed[at : at + TILE]
        turned = both.T
        at += TILE
        diagonal = jnp.broadcast_to(packed[at : at + 1], (TILE, TILE))
        at += 8
        put(i, i, jnp.where(row <= col, both, turned))
        put(i + 1, i + 1, jnp.where(row > col, both, jnp.where(row < col, turned, diagonal)))


def ortho_kernel(
    n, groups, grad, tokens, back, cols, stage, raw, afar, near, acc, full, gout, gin, qout, qin,
    gh, gl, ph, qh, ql, th, tl,
    lsem, fss, frs, nss, nrs, css, crs, dss, drs, ass, ars, bss, brs, tss, trs, gss, grs, own_sem
):
    row, grp = lax.axis_index("row"), lax.axis_index("grp")
    others = [lax.rem(grp + k, groups) for k in range(1, groups)]
    greet(n, groups, others)
    order = far_first(n)
    half = n // 2
    side, seat = row // half, lax.rem(row, half)
    mate = lax.rem(row + half, n)
    near_order = far_first(half)
    top = float(jnp.finfo(bf16).max)

    def peer(k):
        return side * half + lax.rem(seat + k, half)

    def source(k):
        return lax.rem(seat + half - k, half)

    def across(r):
        return lax.rem(r + half, n)

    def remote(src, dst, ss, rs, where):
        copy = pltpu.make_async_remote_copy(
            src_ref=src, dst_ref=dst, send_sem=ss, recv_sem=rs, device_id=where, device_id_type=MESH
        )
        copy.start()
        return copy

    def share_of(to):
        size, wide = cols.shape[2], cols.shape[3]
        down = pl.ds(pl.multiple_of(grp * size, size), size)
        return tokens.at[down, pl.ds(pl.multiple_of(to * wide, wide), wide)]

    plan = [(k, True) for k in near_order] + [(0, True)] + [(k, False) for k in near_order] + [(0, False)]
    loads = []
    for slot, (k, helping) in enumerate(plan):
        index = across(peer(k)) if helping else peer(k)
        load = pltpu.make_async_copy(grad.at[index], stage.at[slot], lsem.at[slot])
        load.start()
        loads.append((index, load))
    fsends, nsends = {}, {}
    for slot, (k, helping) in enumerate(plan):
        index, load = loads[slot]
        load.wait()
        value = jnp.clip(stage[slot], -top, top).astype(bf16)
        if k == 0:
            (afar if helping else near)[seat] = value
            continue
        raw[slot] = value
        if helping:
            fsends[k] = remote(raw.at[slot], afar.at[seat], fss.at[k], frs.at[k], (grp, peer(k)))
        else:
            nsends[k] = remote(raw.at[slot], near.at[seat], nss.at[k], nrs.at[k], (grp, peer(k)))

    acc[...] = dot_t(afar[seat], afar[seat])
    for k in near_order:
        fsends[k].wait_recv()
        acc[...] += dot_t(afar[source(k)], afar[source(k)])
    pack(acc, gout)
    cross = remote(gout, gin, css, crs, (grp, mate))

    tsends = {}
    for k in order:
        to = lax.rem(row + k, n)
        tsends[k] = remote(share_of(to), cols.at[grp, row], tss.at[k], trs.at[k], (grp, to))
    own = pltpu.make_async_copy(share_of(row), cols.at[grp, row], own_sem)
    own.start()

    full[...] = dot_t(near[seat], near[seat])
    for k in near_order:
        nsends[k].wait_recv()
        full[...] += dot_t(near[source(k)], near[source(k)])
    cross.wait_recv()

    def put_sum(i, j, value):
        acc[block(i), block(j)] = value

    pack(full, qout)
    qout[...] = qout[...] + gin[...]
    unpack(qout, put_sum)

    total = acc[...]
    down, right = iotas(total.shape[0])
    eye = down == right
    norm2 = jnp.sum(jnp.where(eye, total, 0.0), keepdims=True)
    scale = 1.0 / (jnp.sqrt(norm2) + 1e-07)
    gh[...], gl[...] = split(jnp.where(norm2 < jnp.inf, scale * (scale * total), 0.0))

    def whole(high, low):
        return high[...].astype(f32) + low[...].astype(f32)

    for turn in range(ITERS):
        ph[...] = (coef_b * gh[...].astype(f32) + coef_c * dot(gh[...], gh[...])).astype(bf16)
        if turn == 0:
            factor = jnp.where(eye, coef_a, 0.0) + ph[...].astype(f32)
        else:
            factor = coef_a * whole(qh, ql) + (dot(qh[...], ph[...]) + dot(ql[...], ph[...]))
        if turn < ITERS - 1:
            qh[...], ql[...] = split(factor)
            th[...], tl[...] = split(coef_a * whole(gh, gl) + (dot(gh[...], ph[...]) + dot(gl[...], ph[...])))
            gh[...], gl[...] = split(coef_a * whole(th, tl) + (dot_t(ph[...], th[...]) + dot_t(ph[...], tl[...])))
        else:
            full[...] = scale * factor
    pack(full, qout)
    recross = remote(qout, qin, dss, drs, (grp, mate))
    qh[...], ql[...] = split(full[...])

    def apply(value):
        return (dot(value, qh[...]) + dot(value, ql[...])).astype(bf16)

    asends, bsends = {}, {}
    for k in near_order:
        at = lax.rem(seat + k, half)
        near[at] = apply(near[at])
        asends[k] = remote(near.at[at], back.at[row], ass.at[k], ars.at[k], (grp, peer(k)))
    back[row] = apply(near[seat])

    own.wait()
    for k in order:
        tsends[k].wait_recv()
    gsends = []
    for j, g in enumerate(others):
        gsends.append(remote(cols.at[grp], cols.at[grp], gss.at[j], grs.at[j], (g, row)))

    recross.wait_recv()

    def put_factor(i, j, value):
        qh[block(i), block(j)], ql[block(i), block(j)] = split(value)

    unpack(qin, put_factor)
    for k in near_order:
        at = lax.rem(seat + k, half)
        afar[at] = apply(afar[at])
        bsends[k] = remote(afar.at[at], back.at[mate], bss.at[k], brs.at[k], (grp, peer(k)))
    back[mate] = apply(afar[seat])
    cross.wait_send()
    recross.wait_send()
    for k in order:
        tsends[k].wait_send()
    for copy in gsends:
        copy.wait()
    for k in near_order:
        fsends[k].wait_send()
        nsends[k].wait_send()
        asends[k].wait()
        bsends[k].wait()


def project_kernel(
    n, groups, index, valid, cols, fresh, out, part, got1, sum1, got2, sum2, got3,
    ss1, rs1, ss2, rs2, ss3, rs3
):
    row, grp = lax.axis_index("row"), lax.axis_index("grp")
    ys = groups // CORES
    y, core = grp // CORES, lax.rem(grp, CORES)
    count, piece = out.shape
    partners = [y * CORES + (1 - core)]
    partners += [lax.rem(y + j, ys) * CORES + core for j in range(1, ys)]
    greet(n, groups, partners)
    order = far_first(n) + [0]

    def remote(src, dst, ss, rs, where):
        copy = pltpu.make_async_remote_copy(
            src_ref=src, dst_ref=dst, send_sem=ss, recv_sem=rs, device_id=where, device_id_type=MESH
        )
        copy.start()
        return copy

    one, two, three = {}, {}, {}

    def stage1(k):
        b = lax.rem(row + k, n)
        tok = cols[:, b].reshape(count, cols.shape[3])
        total = jnp.zeros((count, groups * piece), f32)
        for s in range(MOST):
            term = jnp.dot(tok, fresh[index[b, s]], preferred_element_type=f32)
            total = total + jnp.where(valid[b, s] > 0, term, 0.0)
        total = (total * groups ** (-0.5)).astype(bf16)
        for g in range(groups):
            part[k, g % CORES, g // CORES] = total[:, g * piece : (g + 1) * piece]
        one[k] = remote(part.at[k, 1 - core], got1.at[k], ss1.at[k], rs1.at[k], (partners[0], row))

    def stage2(k):
        one[k].wait_recv()
        two[k] = []
        for j in range(1, ys):
            to = lax.rem(y + j, ys)
            both = part[k, core, to].astype(f32) + got1[k, to].astype(f32)
            sum1[k, j] = both.astype(bf16)
            two[k].append(
                remote(sum1.at[k, j], got2.at[k, j], ss2.at[k, j], rs2.at[k, j], (partners[j], row))
            )

    def stage3(k):
        total = part[k, core, y].astype(f32) + got1[k, y].astype(f32)
        for j in range(1, ys):
            two[k][j - 1].wait_recv()
            total = total + got2[k, j].astype(f32)
        if k == 0:
            return total
        sum2[k] = total.astype(bf16)
        to = lax.rem(row + k, n)
        three[k] = remote(sum2.at[k], got3.at[k], ss3.at[k], rs3.at[k], (grp, to))

    final = None
    lag2, lag3 = LAGS
    for i in range(n + lag3):
        if i < n:
            stage1(order[i])
        if lag2 <= i < n + lag2:
            stage2(order[i - lag2])
        if lag3 <= i < n + lag3:
            final = stage3(order[i - lag3])
    for k in reversed(order[:-1]):
        three[k].wait_recv()
        final = final + got3[k].astype(f32)
    out[...] = final.astype(bf16)
    for k in order:
        one[k].wait_send()
        for copy in two[k]:
            copy.wait_send()
        if k:
            three[k].wait_send()


VM = pl.BlockSpec(memory_space=pltpu.VMEM)
SM = pl.BlockSpec(memory_space=pltpu.SMEM)
ANY = pl.BlockSpec(memory_space=pl.ANY)


def body(grad, weight, owner, tokens, counts):
    ranks = lax.axis_size("row")
    groups = lax.axis_size("grp")
    number, rows, width = grad.shape
    assert number == ranks
    ys = groups // CORES
    dma = pltpu.SemaphoreType.DMA
    count = tokens.shape[0]
    share = count // groups
    half = ranks // 2
    back, cols = pl.pallas_call(
        functools.partial(ortho_kernel, ranks, groups),
        out_shape=[
            jax.ShapeDtypeStruct((ranks, rows, width), bf16),
            jax.ShapeDtypeStruct((groups, ranks, share, rows), bf16),
        ],
        in_specs=[ANY, ANY],
        out_specs=[VM, VM],
        scratch_shapes=[
            pltpu.VMEM((ranks, rows, width), f32),
            pltpu.VMEM((ranks, rows, width), bf16),
            pltpu.VMEM((half, rows, width), bf16),
            pltpu.VMEM((half, rows, width), bf16),
        ]
        + [pltpu.VMEM((width, width), f32)] * 2
        + [pltpu.VMEM((packed_rows(width), TILE), f32)] * 4
        + [pltpu.VMEM((width, width), bf16)] * 7
        + [dma((ranks,))]
        + [dma((half,))] * 4
        + [dma] * 4
        + [dma((half,))] * 4
        + [dma((ranks,))] * 2
        + [dma((groups,))] * 2
        + [dma],
        compiler_params=pltpu.CompilerParams(
            collective_id=0, has_side_effects=True, vmem_limit_bytes=48 * 1024 * 1024
        ),
        name="ortho",
    )(grad, tokens)
    new_weight = (weight.astype(f32) - step_size * back.astype(f32)).astype(bf16)

    target = owner[:, 0]
    before = jnp.arange(number)[None, :] < jnp.arange(number)[:, None]
    same = target[None, :] == target[:, None]
    slot = jnp.sum((same & before).astype(jnp.int32), axis=1)
    hit = (target[None, None, :] == jnp.arange(ranks)[:, None, None]) & (
        slot[None, None, :] == jnp.arange(MOST)[None, :, None]
    )
    index = jnp.sum(hit * jnp.arange(number)[None, None, :], axis=2).astype(jnp.int32)
    valid = jnp.any(hit, axis=2).astype(jnp.int32)

    piece = width // groups
    summed = pl.pallas_call(
        functools.partial(project_kernel, ranks, groups),
        out_shape=jax.ShapeDtypeStruct((count, piece), bf16),
        in_specs=[SM, SM, VM, VM],
        out_specs=VM,
        scratch_shapes=[
            pltpu.VMEM((ranks, CORES, ys, count, piece), bf16),
            pltpu.VMEM((ranks, ys, count, piece), bf16),
            pltpu.VMEM((ranks, ys, count, piece), bf16),
            pltpu.VMEM((ranks, ys, count, piece), bf16),
            pltpu.VMEM((ranks, count, piece), bf16),
            pltpu.VMEM((ranks, count, piece), bf16),
            dma((ranks,)),
            dma((ranks,)),
            dma((ranks, ys)),
            dma((ranks, ys)),
            dma((ranks,)),
            dma((ranks,)),
        ],
        compiler_params=pltpu.CompilerParams(
            collective_id=1, has_side_effects=True, vmem_limit_bytes=48 * 1024 * 1024
        ),
        name="project",
    )(index, valid, cols, new_weight)
    live = jnp.arange(count)[:, None] < counts[0]
    mixed = jnp.where(live, summed, jnp.zeros_like(summed))
    return (new_weight, mixed)


def solution(mesh):
    placed = (
        P("grp", "row", None),
        P("grp", "row", None),
        P("grp", None),
        P("row", None),
        P("row"),
    )
    return jax.shard_map(
        body,
        mesh=mesh,
        in_specs=placed,
        out_specs=(P("grp", "row", None), P("row", "grp")),
        check_vma=False,
    )
```

```python
import functools
import math

import jax
import jax.numpy as jnp
from jax import lax
from jax.experimental import pallas as pl
from jax.experimental.pallas import tpu as pltpu
from jax.sharding import PartitionSpec as P

ITERS = 5
CORES = 2
LAGS = (1, 2, 3)
TILE = 128
PLANES = 4
SPARE = 3 * 1024 * 1024

coef_a = 3.4445
coef_b = -4.775
coef_c = 2.0315
step_size = 0.5

f32 = jnp.float32
bf16 = jnp.bfloat16
MESH = pl.DeviceIdType.MESH


def far_first(n):
    return sorted(range(1, n), key=lambda k: abs(k - n // 2))


def greet(n, groups, grp_shifts):
    row, grp = lax.axis_index("row"), lax.axis_index("grp")
    barrier = pltpu.get_barrier_semaphore()
    for k in range(1, n):
        pl.semaphore_signal(
            barrier, inc=1, device_id=(grp, lax.rem(row + k, n)), device_id_type=MESH
        )
    for g in grp_shifts:
        pl.semaphore_signal(barrier, inc=1, device_id=(g, row), device_id_type=MESH)
    pl.semaphore_wait(barrier, n - 1 + len(grp_shifts))


def split(v):
    high = v.astype(bf16)
    return high, (v - high.astype(f32)).astype(bf16)


def dot(a, b):
    return jnp.dot(a, b, preferred_element_type=f32)


def dot_t(a, b):
    return lax.dot_general(a, b, (((0,), (0,)), ((), ())), preferred_element_type=f32)


def iotas(size):
    shape = (size, size)
    return lax.broadcasted_iota(jnp.int32, shape, 0), lax.broadcasted_iota(jnp.int32, shape, 1)


def block(i):
    return slice(i * TILE, (i + 1) * TILE)


def packed_rows(width):
    count = width // TILE
    return (count * (count - 1) // 2 + count // 2) * TILE + count // 2 * 8


def pack(full, out):
    count = full.shape[0] // TILE
    row, col = iotas(TILE)
    at = 0
    for i in range(count):
        for j in range(i + 1, count):
            out[at : at + TILE] = full[block(i), block(j)]
            at += TILE
    for i in range(0, count, 2):
        one, two = full[block(i), block(i)], full[block(i + 1), block(i + 1)]
        out[at : at + TILE] = jnp.where(row <= col, one, two)
        at += TILE
        diagonal = jnp.sum(jnp.where(row == col, two, 0.0), axis=0, keepdims=True)
        out[at : at + 8] = jnp.broadcast_to(diagonal, (8, TILE))
        at += 8


def unpack(packed, put):
    count = 1
    while packed_rows(count * TILE) < packed.shape[0]:
        count += 1
    row, col = iotas(TILE)
    at = 0
    for i in range(count):
        for j in range(i + 1, count):
            value = packed[at : at + TILE]
            put(i, j, value)
            put(j, i, value.T)
            at += TILE
    for i in range(0, count, 2):
        both = packed[at : at + TILE]
        turned = both.T
        at += TILE
        diagonal = jnp.broadcast_to(packed[at : at + 1], (TILE, TILE))
        at += 8
        put(i, i, jnp.where(row <= col, both, turned))
        put(i + 1, i + 1, jnp.where(row > col, both, jnp.where(row < col, turned, diagonal)))


def step_kernel(
    n, groups, counts, listed, grad, weight, tokens, back, mixed, cols, fresh, old,
    stage, raw, afar, near, acc, full, gout, gin, qout, qin, gh, gl, ph, qh, ql, th, tl,
    part, got1, gotx, goty, sum2, sum3, gotz,
    lsem, fss, frs, nss, nrs, css, crs, dss, drs, ass, ars, bss, brs, tss, trs, gss, grs, own_sem, wsem, owner, osem,
    ss1, rs1, ssx, rsx, ssy, rsy, ssz, rsz
):
    row, grp = lax.axis_index("row"), lax.axis_index("grp")
    others = [lax.rem(grp + k, groups) for k in range(1, groups)]
    greet(n, groups, others)
    order = far_first(n)
    half = n // 2
    side, seat = row // half, lax.rem(row, half)
    near_order = far_first(half)
    top = float(jnp.finfo(bf16).max)

    def peer(k):
        return side * half + lax.rem(seat + k, half)

    def source(k):
        return lax.rem(seat + half - k, half)

    def across(r):
        plane = n // PLANES
        return n - plane - r + 2 * lax.rem(r, plane)

    mate = across(row)

    def remote(src, dst, ss, rs, where):
        copy = pltpu.make_async_remote_copy(
            src_ref=src, dst_ref=dst, send_sem=ss, recv_sem=rs, device_id=where, device_id_type=MESH
        )
        copy.start()
        return copy

    def share_of(to):
        size, wide = cols.shape[2], cols.shape[3]
        down = pl.ds(pl.multiple_of(grp * size, size), size)
        return tokens.at[down, pl.ds(pl.multiple_of(to * wide, wide), wide)]

    plan = [(k, True) for k in near_order] + [(0, True)] + [(k, False) for k in near_order] + [(0, False)]
    loads = []
    for slot, (k, helping) in enumerate(plan):
        index = across(peer(k)) if helping else peer(k)
        load = pltpu.make_async_copy(grad.at[index], stage.at[slot], lsem.at[slot])
        load.start()
        loads.append((index, load))
    fsends, nsends = {}, {}
    for slot, (k, helping) in enumerate(plan):
        index, load = loads[slot]
        load.wait()
        value = jnp.clip(stage[slot], -top, top).astype(bf16)
        if k == 0:
            (afar if helping else near)[seat] = value
            continue
        raw[slot] = value
        if helping:
            fsends[k] = remote(raw.at[slot], afar.at[seat], fss.at[k], frs.at[k], (grp, peer(k)))
        else:
            nsends[k] = remote(raw.at[slot], near.at[seat], nss.at[k], nrs.at[k], (grp, peer(k)))

    fetch = pltpu.make_async_copy(weight, old, wsem)
    fetch.start()
    names = pltpu.make_async_copy(listed, owner, osem)
    names.start()
    acc[...] = dot_t(afar[seat], afar[seat])
    for k in near_order:
        fsends[k].wait_recv()
        acc[...] += dot_t(afar[source(k)], afar[source(k)])
    pack(acc, gout)
    cross = remote(gout, gin, css, crs, (grp, mate))

    full[...] = dot_t(near[seat], near[seat])
    for k in near_order:
        nsends[k].wait_recv()
        full[...] += dot_t(near[source(k)], near[source(k)])
    tsends = {}
    for k in order:
        to = lax.rem(row + k, n)
        tsends[k] = remote(share_of(to), cols.at[grp, row], tss.at[k], trs.at[k], (grp, to))
    own = pltpu.make_async_copy(share_of(row), cols.at[grp, row], own_sem)
    own.start()

    cross.wait_recv()

    def put_sum(i, j, value):
        acc[block(i), block(j)] = value

    pack(full, qout)
    qout[...] = qout[...] + gin[...]
    unpack(qout, put_sum)

    total = acc[...]
    down, right = iotas(total.shape[0])
    eye = down == right
    norm2 = jnp.sum(jnp.where(eye, total, 0.0), keepdims=True)
    scale = 1.0 / (jnp.sqrt(norm2) + 1e-07)
    gh[...], gl[...] = split(jnp.where(norm2 < jnp.inf, scale * (scale * total), 0.0))

    def whole(high, low):
        return high[...].astype(f32) + low[...].astype(f32)

    for turn in range(ITERS):
        ph[...] = (coef_b * gh[...].astype(f32) + coef_c * dot(gh[...], gh[...])).astype(bf16)
        if turn == 0:
            factor = jnp.where(eye, coef_a, 0.0) + ph[...].astype(f32)
        else:
            factor = coef_a * whole(qh, ql) + (dot(qh[...], ph[...]) + dot(ql[...], ph[...]))
        if turn < ITERS - 1:
            qh[...], ql[...] = split(factor)
            th[...], tl[...] = split(coef_a * whole(gh, gl) + (dot(gh[...], ph[...]) + dot(gl[...], ph[...])))
            gh[...], gl[...] = split(coef_a * whole(th, tl) + (dot_t(ph[...], th[...]) + dot_t(ph[...], tl[...])))
        else:
            full[...] = scale * factor
    pack(full, qout)
    recross = remote(qout, qin, dss, drs, (grp, mate))
    qh[...], ql[...] = split(full[...])

    def apply(value):
        return (dot(value, qh[...]) + dot(value, ql[...])).astype(bf16)

    asends, bsends = {}, {}
    for k in near_order:
        at = lax.rem(seat + k, half)
        near[at] = apply(near[at])
        asends[k] = remote(near.at[at], back.at[row], ass.at[k], ars.at[k], (grp, peer(k)))
    back[row] = apply(near[seat])

    own.wait()
    for k in order:
        tsends[k].wait_recv()
    gsends = []
    for j, g in enumerate(others):
        gsends.append(remote(cols.at[grp], cols.at[grp], gss.at[j], grs.at[j], (g, row)))

    recross.wait_recv()

    def put_factor(i, j, value):
        qh[block(i), block(j)], ql[block(i), block(j)] = split(value)

    unpack(qin, put_factor)
    for k in near_order:
        at = lax.rem(seat + k, half)
        afar[at] = apply(afar[at])
        bsends[k] = remote(afar.at[at], back.at[mate], bss.at[k], brs.at[k], (grp, peer(k)))
    back[mate] = apply(afar[seat])
    fetch.wait()
    names.wait()

    def renew(index):
        fresh[index] = (old[index].astype(f32) - step_size * back[index].astype(f32)).astype(bf16)

    renew(row)
    for k in near_order:
        asends[k].wait_recv()
        renew(side * half + source(k))
    renew(mate)
    for copy in gsends:
        copy.wait_recv()
    for k in near_order:
        bsends[k].wait_recv()
        renew(across(side * half + source(k)))

    project(
        n, groups, remote, owner, counts, fresh, mixed, cols, part, got1, gotx, goty, sum2, sum3, gotz,
        ss1, rs1, ssx, rsx, ssy, rsy, ssz, rsz
    )
    cross.wait_send()
    recross.wait_send()
    for k in order:
        tsends[k].wait_send()
    for copy in gsends:
        copy.wait_send()
    for k in near_order:
        fsends[k].wait_send()
        nsends[k].wait_send()
        asends[k].wait_send()
        bsends[k].wait_send()


def project(
    n, groups, remote, owner, counts, fresh, mixed, cols, part, got1, gotx, goty, sum2, sum3, gotz,
    ss1, rs1, ssx, rsx, ssy, rsy, ssz, rsz
):
    row, grp = lax.axis_index("row"), lax.axis_index("grp")
    lanes, ys = n // PLANES, groups // CORES
    z, x = row // lanes, lax.rem(row, lanes)
    y, core = grp // CORES, lax.rem(grp, CORES)
    count, piece = mixed.shape
    order = far_first(PLANES) + [0]
    one, two, three, four = {}, {}, {}, {}

    def matrices_of(b):
        first, last = jnp.int32(n), jnp.int32(-1)
        for e in range(n):
            hit = owner[e] == b
            first = jnp.minimum(first, jnp.where(hit, e, n))
            last = jnp.maximum(last, jnp.where(hit, e, -1))
        return first, last

    def stage1(turn):
        k = order[turn]
        for j in range(lanes):
            b = lax.rem(z + k, PLANES) * lanes + lax.rem(x + j, lanes)
            first, last = matrices_of(b)
            tok = cols[:, b].reshape(count, cols.shape[3])
            total = jnp.where(last >= 0, dot(tok, fresh[jnp.minimum(first, n - 1)]), 0.0)
            total = total + jnp.where(last > first, dot(tok, fresh[jnp.maximum(last, 0)]), 0.0)
            total = (total * groups ** (-0.5)).astype(bf16)
            for g in range(groups):
                part[k, g % CORES, j, g // CORES] = total[:, g * piece : (g + 1) * piece]
        one[k] = remote(part.at[k, 1 - core], got1.at[k], ss1.at[k], rs1.at[k], (y * CORES + 1 - core, row))

    def to_x(k, j, src, dst):
        where = (grp, z * lanes + lax.rem(x + j, lanes))
        return remote(src, dst, ssx.at[k, j], rsx.at[k, j], where)

    def to_y(k, j, src, dst):
        where = (lax.rem(y + j, ys) * CORES + core, row)
        return remote(src, dst, ssy.at[k, j], rsy.at[k, j], where)

    def stage2(turn):
        k = order[turn]
        one[k].wait_recv()
        two[k] = []
        for j in range(lanes):
            for i in range(ys):
                at = lax.rem(y + i, ys)
                got1[k, j, at] = (part[k, core, j, at].astype(f32) + got1[k, j, at].astype(f32)).astype(bf16)
        if turn % 2 == 0:
            for j in range(1, lanes):
                two[k].append(to_x(k, j, got1.at[k, j], gotx.at[k, j]))
        else:
            for i in range(1, ys):
                two[k].append(to_y(k, i, got1.at[k, :, lax.rem(y + i, ys)], goty.at[k, i]))

    def stage3(turn):
        k = order[turn]
        three[k] = []
        for copy in two[k]:
            copy.wait_recv()
        if turn % 2 == 0:
            for i in reversed(range(ys)):
                at = lax.rem(y + i, ys)
                total = got1[k, 0, at].astype(f32)
                for j in range(1, lanes):
                    total = total + gotx[k, j, at].astype(f32)
                sum2[k, i] = total.astype(bf16)
                if i:
                    three[k].append(to_y(k, i, sum2.at[k, i], goty.at[k, i, 0]))
        else:
            for j in reversed(range(lanes)):
                total = got1[k, j, y].astype(f32)
                for i in range(1, ys):
                    total = total + goty[k, i, j].astype(f32)
                sum2[k, j] = total.astype(bf16)
                if j:
                    three[k].append(to_x(k, j, sum2.at[k, j], gotx.at[k, j, 0]))

    def stage4(turn):
        k = order[turn]
        for copy in three[k]:
            copy.wait_recv()
        total = sum2[k, 0].astype(f32)
        if turn % 2 == 0:
            for i in range(1, ys):
                total = total + goty[k, i, 0].astype(f32)
        else:
            for j in range(1, lanes):
                total = total + gotx[k, j, 0].astype(f32)
        if k == 0:
            return total
        sum3[k] = total.astype(bf16)
        four[k] = remote(
            sum3.at[k], gotz.at[k], ssz.at[k], rsz.at[k], (grp, lax.rem(z + k, PLANES) * lanes + x)
        )

    final = None
    for turn in range(PLANES + LAGS[2]):
        if turn < PLANES:
            stage1(turn)
        for stage, lag in zip((stage2, stage3, stage4), LAGS):
            if lag <= turn < PLANES + lag:
                final = stage(turn - lag)
    for k in order[:-1]:
        four[k].wait_recv()
        final = final + gotz[k].astype(f32)
    live = lax.broadcasted_iota(jnp.int32, (count, piece), 0) < counts[0]
    mixed[...] = jnp.where(live, final, 0.0).astype(bf16)
    for k in order:
        for copy in [one[k]] + two[k] + three[k]:
            copy.wait_send()
        if k:
            four[k].wait_send()


VM = pl.BlockSpec(memory_space=pltpu.VMEM)
SM = pl.BlockSpec(memory_space=pltpu.SMEM)
HBM = pl.BlockSpec(memory_space=pltpu.HBM)


def body(grad, weight, owner, tokens, counts):
    ranks = lax.axis_size("row")
    groups = lax.axis_size("grp")
    number, rows, width = grad.shape
    assert number == ranks
    half = ranks // 2
    lanes, ys = ranks // PLANES, groups // CORES
    count = tokens.shape[0]
    share, piece = count // groups, width // groups
    dma = pltpu.SemaphoreType.DMA
    vmem = pltpu.VMEM
    packed = vmem((packed_rows(width), TILE), f32)
    buffers = [
        vmem((groups, ranks, share, rows), bf16),
        vmem((ranks, rows, width), bf16),
        vmem((ranks, rows, width), bf16),
        vmem((ranks, rows, width), f32),
        vmem((ranks, rows, width), bf16),
        vmem((half, rows, width), bf16),
        vmem((half, rows, width), bf16),
    ]
    buffers += [vmem((width, width), f32)] * 2
    buffers += [packed] * 4
    buffers += [vmem((width, width), bf16)] * 7
    buffers += [
        vmem((PLANES, CORES, lanes, ys, count, piece), bf16),
        vmem((PLANES, lanes, ys, count, piece), bf16),
        vmem((PLANES, lanes, ys, count, piece), bf16),
        vmem((PLANES, ys, lanes, count, piece), bf16),
        vmem((PLANES, max(ys, lanes), count, piece), bf16),
        vmem((PLANES, count, piece), bf16),
        vmem((PLANES, count, piece), bf16),
    ]
    semaphores = [dma((ranks,))]
    semaphores += [dma((half,))] * 4
    semaphores += [dma] * 4
    semaphores += [dma((half,))] * 4
    semaphores += [dma((ranks,))] * 2
    semaphores += [dma((groups,))] * 2
    semaphores += [dma] * 2
    semaphores += [pltpu.SMEM((number,), jnp.int32), dma]
    semaphores += [dma((PLANES,))] * 2
    semaphores += [dma((PLANES, lanes))] * 2
    semaphores += [dma((PLANES, ys))] * 2
    semaphores += [dma((PLANES,))] * 2
    lane = 128
    held = sum(
        math.prod(b.shape[:-1]) * pl.cdiv(b.shape[-1], lane) * lane * jnp.dtype(b.dtype).itemsize for b in buffers
    )
    back, mixed = pl.pallas_call(
        functools.partial(step_kernel, ranks, groups),
        out_shape=[
            jax.ShapeDtypeStruct((ranks, rows, width), bf16),
            jax.ShapeDtypeStruct((count, piece), bf16),
        ],
        in_specs=[SM, HBM, HBM, HBM, HBM],
        out_specs=[VM, VM],
        scratch_shapes=buffers + semaphores,
        compiler_params=pltpu.CompilerParams(
            collective_id=0, has_side_effects=True, vmem_limit_bytes=held + SPARE
        ),
        name="step",
    )(counts, *[pltpu.with_memory_space_constraint(a, pltpu.HBM) for a in (owner[:, 0], grad, weight, tokens)])
    new_weight = (weight.astype(f32) - step_size * back.astype(f32)).astype(bf16)
    return new_weight, mixed


def solution(mesh):
    placed = (
        P("grp", "row", None),
        P("grp", "row", None),
        P("grp", None),
        P("row", None),
        P("row"),
    )
    return jax.shard_map(
        body,
        mesh=mesh,
        in_specs=placed,
        out_specs=(P("grp", "row", None), P("row", "grp")),
        check_vma=False,
    )
```

```python
import functools
import math

import jax
import jax.numpy as jnp
from jax import lax
from jax.experimental import pallas as pl
from jax.experimental.pallas import tpu as pltpu
from jax.sharding import PartitionSpec as P

ITERS = 5
CORES = 2
LAGS = (1, 3, 5)
TILE = 128
PAD = 16
PLANES = 4
SPARE = 3 * 1024 * 1024

coef_a = 3.4445
coef_b = -4.775
coef_c = 2.0315
step_size = 0.5

f32 = jnp.float32
bf16 = jnp.bfloat16
MESH = pl.DeviceIdType.MESH


def far_first(n):
    return sorted(range(1, n), key=lambda k: abs(k - n // 2))


def greet(n, groups, grp_shifts):
    row, grp = lax.axis_index("row"), lax.axis_index("grp")
    barrier = pltpu.get_barrier_semaphore()
    for k in range(1, n):
        pl.semaphore_signal(
            barrier, inc=1, device_id=(grp, lax.rem(row + k, n)), device_id_type=MESH
        )
    for g in grp_shifts:
        pl.semaphore_signal(barrier, inc=1, device_id=(g, row), device_id_type=MESH)
    pl.semaphore_wait(barrier, n - 1 + len(grp_shifts))


def split(v):
    high = v.astype(bf16)
    return high, (v - high.astype(f32)).astype(bf16)


def dot(a, b):
    return jnp.dot(a, b, preferred_element_type=f32)


def dot_t(a, b):
    return lax.dot_general(a, b, (((0,), (0,)), ((), ())), preferred_element_type=f32)


def iotas(size):
    shape = (size, size)
    return lax.broadcasted_iota(jnp.int32, shape, 0), lax.broadcasted_iota(jnp.int32, shape, 1)


def block(i):
    return slice(i * TILE, (i + 1) * TILE)


def packed_rows(width):
    count = width // TILE
    return (count * (count - 1) // 2 + count // 2) * TILE + count // 2 * PAD


def layout_of(width):
    count = width // TILE
    middle = count // 2
    items, at, left = [], 0, 0
    for low, high in ((0, middle), (middle, count)):
        for i in range(low, high):
            for j in range(i + 1, count):
                items.append((at, i, j))
                at += TILE
        for i in range(low, high, 2):
            items.append((at, i, i))
            at += TILE + PAD
        left = left or at
    return items, left


def pack(full, out):
    row, col = iotas(TILE)
    for at, i, j in layout_of(full.shape[0])[0]:
        if i < j:
            out[at : at + TILE] = full[block(i), block(j)].astype(out.dtype)
            continue
        one, two = full[block(i), block(i)], full[block(i + 1), block(i + 1)]
        out[at : at + TILE] = jnp.where(row <= col, one, two).astype(out.dtype)
        diagonal = jnp.sum(jnp.where(row == col, two, 0.0), axis=0, keepdims=True)
        out[at + TILE : at + TILE + PAD] = jnp.broadcast_to(diagonal, (PAD, TILE)).astype(out.dtype)


def unpack(packed, width, put, low, high):
    row, col = iotas(TILE)
    for at, i, j in layout_of(width)[0]:
        if not low <= at < high:
            continue
        value = packed[at : at + TILE].astype(f32)
        turned = value.T
        if i < j:
            put(i, j, value)
            put(j, i, turned)
            continue
        diagonal = jnp.broadcast_to(packed[at + TILE : at + TILE + PAD].astype(f32)[:1], (TILE, TILE))
        put(i, i, jnp.where(row <= col, value, turned))
        put(i + 1, i + 1, jnp.where(row > col, value, jnp.where(row < col, turned, diagonal)))


def step_kernel(
    n, groups, counts, listed, grad, weight, tokens, fresh, mixed, cols, back, old,
    stage, raw, afar, near, update, acc, full, gout, gin, gsum, qout, qin, dout, din, gh, gl, ph, qh, ql, th, tl,
    part, got1, gotx, goty, sum2, sum3, gotz,
    lsem, fss, frs, nss, nrs, css, crs, dss, drs, ass, ars, bss, brs, tss, trs, gss, grs, own_sem, wsem, owner, osem, ess, ers,
    ss1, rs1, ssx, rsx, ssy, rsy, ssz, rsz
):
    row, grp = lax.axis_index("row"), lax.axis_index("grp")
    others = [lax.rem(grp + k, groups) for k in range(1, groups)]
    order = far_first(n)
    half = n // 2
    side, seat = row // half, lax.rem(row, half)
    near_order = far_first(half)
    top = float(jnp.finfo(bf16).max)
    width = acc.shape[0]
    left = layout_of(width)[1]
    pieces = ((0, left), (left, qout.shape[0]))

    def peer(k):
        return side * half + lax.rem(seat + k, half)

    def source(k):
        return lax.rem(seat + half - k, half)

    def across(r):
        plane = n // PLANES
        return n - plane - r + 2 * lax.rem(r, plane)

    mate = across(row)

    def remote(src, dst, ss, rs, where):
        copy = pltpu.make_async_remote_copy(
            src_ref=src, dst_ref=dst, send_sem=ss, recv_sem=rs, device_id=where, device_id_type=MESH
        )
        copy.start()
        return copy

    def share_of(to):
        size, wide = cols.shape[2], cols.shape[3]
        down = pl.ds(pl.multiple_of(grp * size, size), size)
        return tokens.at[down, pl.ds(pl.multiple_of(to * wide, wide), wide)]

    plan = [(k, True) for k in near_order] + [(0, True)] + [(k, False) for k in near_order] + [(0, False)]
    loads = []
    for slot, (k, helping) in enumerate(plan):
        index = across(peer(k)) if helping else peer(k)
        load = pltpu.make_async_copy(grad.at[index], stage.at[slot], lsem.at[slot])
        load.start()
        loads.append((index, load))
    greet(n, groups, others)
    fsends, nsends = {}, {}
    for slot, (k, helping) in enumerate(plan):
        index, load = loads[slot]
        load.wait()
        value = jnp.clip(stage[slot], -top, top).astype(bf16)
        if k == 0:
            (afar if helping else near)[seat] = value
            continue
        raw[slot] = value
        if helping:
            fsends[k] = remote(raw.at[slot], afar.at[seat], fss.at[k], frs.at[k], (grp, peer(k)))
        else:
            nsends[k] = remote(raw.at[slot], near.at[seat], nss.at[k], nrs.at[k], (grp, peer(k)))

    fetch = pltpu.make_async_copy(weight, old, wsem)
    fetch.start()
    names = pltpu.make_async_copy(listed, owner, osem)
    names.start()
    acc[...] = dot_t(afar[seat], afar[seat])
    for k in near_order:
        fsends[k].wait_recv()
        acc[...] += dot_t(afar[source(k)], afar[source(k)])
    pack(acc, gout)
    cross = remote(gout, gin, css, crs, (grp, mate))

    full[...] = dot_t(near[seat], near[seat])
    for k in near_order:
        nsends[k].wait_recv()
        full[...] += dot_t(near[source(k)], near[source(k)])
    tsends = {}
    for k in order:
        to = lax.rem(row + k, n)
        tsends[k] = remote(share_of(to), cols.at[grp, row], tss.at[k], trs.at[k], (grp, to))
    own = pltpu.make_async_copy(share_of(row), cols.at[grp, row], own_sem)
    own.start()

    cross.wait_recv()

    def put_sum(i, j, value):
        acc[block(i), block(j)] = value

    pack(full, gsum)
    gsum[...] = gsum[...] + gin[...]
    unpack(gsum, width, put_sum, 0, gsum.shape[0])

    total = acc[...]
    down, right = iotas(total.shape[0])
    eye = down == right
    norm2 = jnp.sum(jnp.where(eye, total, 0.0), keepdims=True)
    scale = 1.0 / (jnp.sqrt(norm2) + 1e-07)
    gh[...], gl[...] = split(jnp.where(norm2 < jnp.inf, scale * (scale * total), 0.0))

    def whole(high, low):
        return high[...].astype(f32) + low[...].astype(f32)

    for turn in range(ITERS):
        ph[...] = (coef_b * gh[...].astype(f32) + coef_c * dot(gh[...], gh[...])).astype(bf16)
        if turn == 0:
            factor = jnp.where(eye, coef_a, 0.0) + ph[...].astype(f32)
        else:
            factor = coef_a * whole(qh, ql) + (dot(qh[...], ph[...]) + dot(ql[...], ph[...]))
        if turn < ITERS - 1:
            qh[...], ql[...] = split(factor)
            th[...], tl[...] = split(coef_a * whole(gh, gl) + (dot(gh[...], ph[...]) + dot(gl[...], ph[...])))
            gh[...], gl[...] = split(coef_a * whole(th, tl) + (dot_t(ph[...], th[...]) + dot_t(ph[...], tl[...])))
        else:
            factor = scale * factor
            diagonal = jnp.sum(jnp.where(eye, factor, 0.0), axis=0, keepdims=True)
            dout[...] = jnp.broadcast_to(diagonal, dout.shape)
            full[...] = jnp.where(eye, 0.0, factor)
    pack(full, qout)
    outline = remote(dout, din, ess, ers, (grp, mate))
    recross = []
    for part_of, (low, high) in enumerate(pieces):
        rows = pl.ds(low, high - low)
        recross.append(remote(qout.at[rows], qin.at[rows], dss.at[part_of], drs.at[part_of], (grp, mate)))
    qh[...] = full[...].astype(bf16)

    def apply(value, columns, diagonal):
        return (value[:, columns].astype(f32) * diagonal[:1, columns] + dot(value, qh[:, columns])).astype(bf16)

    asends, bsends = {}, {}
    for k in near_order:
        at = lax.rem(seat + k, half)
        near[at] = apply(near[at], slice(None), dout)
        asends[k] = remote(near.at[at], back.at[row], ass.at[k], ars.at[k], (grp, peer(k)))
    back[row] = apply(near[seat], slice(None), dout)

    own.wait()
    for k in order:
        tsends[k].wait_recv()
    gsends = []
    for j, g in enumerate(others):
        gsends.append(remote(cols.at[grp], cols.at[grp], gss.at[j], grs.at[j], (g, row)))

    def put_factor(i, j, value):
        qh[block(i), block(j)] = value.astype(bf16)

    outline.wait_recv()
    for part_of, (low, high) in enumerate(pieces):
        recross[part_of].wait_recv()
        unpack(qin, width, put_factor, low, high)
        columns = slice(part_of * width // 2, (part_of + 1) * width // 2)
        for k in near_order:
            at = lax.rem(seat + k, half)
            update[at, :, columns] = apply(afar[at], columns, din)
            bsends[part_of, k] = remote(
                update.at[at, :, columns], back.at[mate, :, columns],
                bss.at[part_of, k], brs.at[part_of, k], (grp, peer(k))
            )
    back[mate] = apply(afar[seat], slice(None), din)
    fetch.wait()
    names.wait()

    def renew(index):
        fresh[index] = (old[index].astype(f32) - step_size * back[index].astype(f32)).astype(bf16)

    renew(row)
    for k in near_order:
        asends[k].wait_recv()
        renew(side * half + source(k))
    renew(mate)
    for copy in gsends:
        copy.wait_recv()
    for k in near_order:
        bsends[0, k].wait_recv()
        bsends[1, k].wait_recv()
        renew(across(side * half + source(k)))

    project(
        n, groups, remote, owner, counts, fresh, mixed, cols, part, got1, gotx, goty, sum2, sum3, gotz,
        ss1, rs1, ssx, rsx, ssy, rsy, ssz, rsz
    )
    cross.wait_send()
    for copy in recross + [outline]:
        copy.wait_send()
    for k in order:
        tsends[k].wait_send()
    for copy in gsends:
        copy.wait_send()
    for k in near_order:
        fsends[k].wait_send()
        nsends[k].wait_send()
        asends[k].wait_send()
        bsends[0, k].wait_send()
        bsends[1, k].wait_send()


def project(
    n, groups, remote, owner, counts, fresh, mixed, cols, part, got1, gotx, goty, sum2, sum3, gotz,
    ss1, rs1, ssx, rsx, ssy, rsy, ssz, rsz
):
    row, grp = lax.axis_index("row"), lax.axis_index("grp")
    lanes, ys = n // PLANES, groups // CORES
    z, x = row // lanes, lax.rem(row, lanes)
    y, core = grp // CORES, lax.rem(grp, CORES)
    count, piece = mixed.shape
    order = far_first(PLANES) + [0]
    one, two, three, four = {}, {}, {}, {}

    def matrices_of(b):
        first, last = jnp.int32(n), jnp.int32(-1)
        for e in range(n):
            hit = owner[e] == b
            first = jnp.minimum(first, jnp.where(hit, e, n))
            last = jnp.maximum(last, jnp.where(hit, e, -1))
        return first, last

    def stage1(turn):
        k = order[turn]
        for j in range(lanes):
            b = lax.rem(z + k, PLANES) * lanes + lax.rem(x + j, lanes)
            first, last = matrices_of(b)
            tok = cols[:, b].reshape(count, cols.shape[3])
            total = jnp.where(last >= 0, dot(tok, fresh[jnp.minimum(first, n - 1)]), 0.0)
            total = total + jnp.where(last > first, dot(tok, fresh[jnp.maximum(last, 0)]), 0.0)
            total = (total * groups ** (-0.5)).astype(bf16)
            for g in range(groups):
                part[k, g % CORES, j, g // CORES] = total[:, g * piece : (g + 1) * piece]
        one[k] = remote(part.at[k, 1 - core], got1.at[k], ss1.at[k], rs1.at[k], (y * CORES + 1 - core, row))

    def to_x(k, j, src, dst):
        where = (grp, z * lanes + lax.rem(x + j, lanes))
        return remote(src, dst, ssx.at[k, j], rsx.at[k, j], where)

    def to_y(k, j, src, dst):
        where = (lax.rem(y + j, ys) * CORES + core, row)
        return remote(src, dst, ssy.at[k, j], rsy.at[k, j], where)

    def stage2(turn):
        k = order[turn]
        one[k].wait_recv()
        two[k] = []
        for j in range(lanes):
            for i in range(ys):
                at = lax.rem(y + i, ys)
                got1[k, j, at] = (part[k, core, j, at].astype(f32) + got1[k, j, at].astype(f32)).astype(bf16)
        if turn % 2 == 0:
            for j in range(1, lanes):
                two[k].append(to_x(k, j, got1.at[k, j], gotx.at[k, j]))
        else:
            for i in range(1, ys):
                two[k].append(to_y(k, i, got1.at[k, :, lax.rem(y + i, ys)], goty.at[k, i]))

    def stage3(turn):
        k = order[turn]
        three[k] = []
        for copy in two[k]:
            copy.wait_recv()
        if turn % 2 == 0:
            for i in reversed(range(ys)):
                at = lax.rem(y + i, ys)
                total = got1[k, 0, at].astype(f32)
                for j in range(1, lanes):
                    total = total + gotx[k, j, at].astype(f32)
                sum2[k, i] = total.astype(bf16)
                if i:
                    three[k].append(to_y(k, i, sum2.at[k, i], goty.at[k, i, 0]))
        else:
            for j in reversed(range(lanes)):
                total = got1[k, j, y].astype(f32)
                for i in range(1, ys):
                    total = total + goty[k, i, j].astype(f32)
                sum2[k, j] = total.astype(bf16)
                if j:
                    three[k].append(to_x(k, j, sum2.at[k, j], gotx.at[k, j, 0]))

    def stage4(turn):
        k = order[turn]
        for copy in three[k]:
            copy.wait_recv()
        total = sum2[k, 0].astype(f32)
        if turn % 2 == 0:
            for i in range(1, ys):
                total = total + goty[k, i, 0].astype(f32)
        else:
            for j in range(1, lanes):
                total = total + gotx[k, j, 0].astype(f32)
        if k == 0:
            return total
        sum3[k] = total.astype(bf16)
        four[k] = remote(
            sum3.at[k], gotz.at[k], ssz.at[k], rsz.at[k], (grp, lax.rem(z + k, PLANES) * lanes + x)
        )

    final = None
    for turn in range(PLANES + LAGS[2]):
        if turn < PLANES:
            stage1(turn)
        for stage, lag in zip((stage2, stage3, stage4), LAGS):
            if lag <= turn < PLANES + lag:
                final = stage(turn - lag)
    for k in order[:-1]:
        four[k].wait_recv()
        final = final + gotz[k].astype(f32)
    live = lax.broadcasted_iota(jnp.int32, (count, piece), 0) < counts[0]
    mixed[...] = jnp.where(live, final, 0.0).astype(bf16)
    for k in order:
        for copy in [one[k]] + two[k] + three[k]:
            copy.wait_send()
        if k:
            four[k].wait_send()


def store_kernel(fresh, mixed, new_weight, out, fsem, msem):
    copies = [pltpu.make_async_copy(mixed, out, msem)]
    for i in range(fresh.shape[0]):
        copies.append(pltpu.make_async_copy(fresh.at[i], new_weight.at[i], fsem.at[i]))
    for copy in copies:
        copy.start()
    for copy in copies:
        copy.wait()


VM = pl.BlockSpec(memory_space=pltpu.VMEM)
SM = pl.BlockSpec(memory_space=pltpu.SMEM)
HBM = pl.BlockSpec(memory_space=pltpu.HBM)


def body(grad, weight, owner, tokens, counts):
    ranks = lax.axis_size("row")
    groups = lax.axis_size("grp")
    number, rows, width = grad.shape
    assert number == ranks
    half = ranks // 2
    lanes, ys = ranks // PLANES, groups // CORES
    count = tokens.shape[0]
    share, piece = count // groups, width // groups
    dma = pltpu.SemaphoreType.DMA
    vmem = pltpu.VMEM
    packed = vmem((packed_rows(width), TILE), f32)
    buffers = [
        vmem((groups, ranks, share, rows), bf16),
        vmem((ranks, rows, width), bf16),
        vmem((ranks, rows, width), bf16),
        vmem((ranks, rows, width), f32),
        vmem((ranks, rows, width), bf16),
        vmem((half, rows, width), bf16),
        vmem((half, rows, width), bf16),
        vmem((half, rows, width), bf16),
    ]
    buffers += [vmem((width, width), f32)] * 2
    buffers += [packed] * 3
    buffers += [vmem((packed_rows(width), TILE), bf16)] * 2
    buffers += [vmem((8, width), f32)] * 2
    buffers += [vmem((width, width), bf16)] * 7
    buffers += [
        vmem((PLANES, CORES, lanes, ys, count, piece), bf16),
        vmem((PLANES, lanes, ys, count, piece), bf16),
        vmem((PLANES, lanes, ys, count, piece), bf16),
        vmem((PLANES, ys, lanes, count, piece), bf16),
        vmem((PLANES, max(ys, lanes), count, piece), bf16),
        vmem((PLANES, count, piece), bf16),
        vmem((PLANES, count, piece), bf16),
    ]
    semaphores = [dma((ranks,))]
    semaphores += [dma((half,))] * 4
    semaphores += [dma] * 2
    semaphores += [dma((2,))] * 2
    semaphores += [dma((half,))] * 2
    semaphores += [dma((2, half))] * 2
    semaphores += [dma((ranks,))] * 2
    semaphores += [dma((groups,))] * 2
    semaphores += [dma] * 2
    semaphores += [pltpu.SMEM((number,), jnp.int32), dma]
    semaphores += [dma] * 2
    semaphores += [dma((PLANES,))] * 2
    semaphores += [dma((PLANES, lanes))] * 2
    semaphores += [dma((PLANES, ys))] * 2
    semaphores += [dma((PLANES,))] * 2
    lane = 128
    held = sum(
        math.prod(b.shape[:-1]) * pl.cdiv(b.shape[-1], lane) * lane * jnp.dtype(b.dtype).itemsize for b in buffers
    )
    fresh, mixed = pl.pallas_call(
        functools.partial(step_kernel, ranks, groups),
        out_shape=[
            jax.ShapeDtypeStruct((ranks, rows, width), bf16),
            jax.ShapeDtypeStruct((count, piece), bf16),
        ],
        in_specs=[SM, HBM, HBM, HBM, HBM],
        out_specs=[VM, VM],
        scratch_shapes=buffers + semaphores,
        compiler_params=pltpu.CompilerParams(
            collective_id=0, has_side_effects=True, vmem_limit_bytes=held + SPARE
        ),
        name="step",
    )(counts, *[pltpu.with_memory_space_constraint(a, pltpu.HBM) for a in (owner[:, 0], grad, weight, tokens)])
    return pl.pallas_call(
        store_kernel,
        out_shape=[jax.ShapeDtypeStruct(a.shape, bf16) for a in (fresh, mixed)],
        in_specs=[VM, VM],
        out_specs=[HBM, HBM],
        scratch_shapes=[dma((ranks,)), dma],
        compiler_params=pltpu.CompilerParams(vmem_limit_bytes=SPARE),
        name="store",
    )(fresh, mixed)


def solution(mesh):
    placed = (
        P("grp", "row", None),
        P("grp", "row", None),
        P("grp", None),
        P("row", None),
        P("row"),
    )
    return jax.shard_map(
        body,
        mesh=mesh,
        in_specs=placed,
        out_specs=(P("grp", "row", None), P("row", "grp")),
        check_vma=False,
    )
```

```python
import functools
import math

import jax
import jax.numpy as jnp
from jax import lax
from jax.experimental import pallas as pl
from jax.experimental.pallas import tpu as pltpu
from jax.sharding import PartitionSpec as P

ITERS = 5
CORES = 2
LAGS = (2, 4)
TILE = 128
PAD = 16
PLANES = 4
SPARE = 3 * 1024 * 1024

coef_a = 3.4445
coef_b = -4.775
coef_c = 2.0315
step_size = 0.5

f32 = jnp.float32
bf16 = jnp.bfloat16
MESH = pl.DeviceIdType.MESH


def far_first(n):
    return sorted(range(1, n), key=lambda k: abs(k - n // 2))


def greet(n, groups, grp_shifts):
    row, grp = lax.axis_index("row"), lax.axis_index("grp")
    barrier = pltpu.get_barrier_semaphore()
    for k in range(1, n):
        pl.semaphore_signal(
            barrier, inc=1, device_id=(grp, lax.rem(row + k, n)), device_id_type=MESH
        )
    for g in grp_shifts:
        pl.semaphore_signal(barrier, inc=1, device_id=(g, row), device_id_type=MESH)
    pl.semaphore_wait(barrier, n - 1 + len(grp_shifts))


def split(v):
    high = v.astype(bf16)
    return high, (v - high.astype(f32)).astype(bf16)


def dot(a, b):
    return jnp.dot(a, b, preferred_element_type=f32)


def dot_t(a, b):
    return lax.dot_general(a, b, (((0,), (0,)), ((), ())), preferred_element_type=f32)


def iotas(size):
    shape = (size, size)
    return lax.broadcasted_iota(jnp.int32, shape, 0), lax.broadcasted_iota(jnp.int32, shape, 1)


def block(i):
    return slice(i * TILE, (i + 1) * TILE)


def packed_rows(width):
    count = width // TILE
    return (count * (count - 1) // 2 + count // 2) * TILE + count // 2 * PAD


def layout_of(width):
    count = width // TILE
    middle = count // 2
    items, at, left = [], 0, 0
    for low, high in ((0, middle), (middle, count)):
        for i in range(low, high):
            for j in range(i + 1, count):
                items.append((at, i, j))
                at += TILE
        for i in range(low, high, 2):
            items.append((at, i, i))
            at += TILE + PAD
        left = left or at
    return items, left


def pack(full, out):
    row, col = iotas(TILE)
    for at, i, j in layout_of(full.shape[0])[0]:
        if i < j:
            out[at : at + TILE] = full[block(i), block(j)].astype(out.dtype)
            continue
        one, two = full[block(i), block(i)], full[block(i + 1), block(i + 1)]
        out[at : at + TILE] = jnp.where(row <= col, one, two).astype(out.dtype)
        diagonal = jnp.sum(jnp.where(row == col, two, 0.0), axis=0, keepdims=True)
        out[at + TILE : at + TILE + PAD] = jnp.broadcast_to(diagonal, (PAD, TILE)).astype(out.dtype)


def unpack(packed, width, put, low, high):
    row, col = iotas(TILE)
    for at, i, j in layout_of(width)[0]:
        if not low <= at < high:
            continue
        value = packed[at : at + TILE].astype(f32)
        turned = value.T
        if i < j:
            put(i, j, value)
            put(j, i, turned)
            continue
        diagonal = jnp.broadcast_to(packed[at + TILE : at + TILE + PAD].astype(f32)[:1], (TILE, TILE))
        put(i, i, jnp.where(row <= col, value, turned))
        put(i + 1, i + 1, jnp.where(row > col, value, jnp.where(row < col, turned, diagonal)))


def step_kernel(
    n, groups, counts, listed, grad, weight, tokens, fresh, mixed, cols, back, old,
    stage, raw, afar, near, update, acc, full, gout, gin, gsum, qout, qin, dout, din, gh, gl, ph, qh, ql, th, tl,
    mine, theirs, given, got1, gotx, goty, sum2, sum3, gotz,
    lsem, fss, frs, nss, nrs, css, crs, dss, drs, ass, ars, bss, brs, tss, trs, gss, grs, own_sem, wsem, owner, osem, ess, ers,
    theirs_of, oss, ors, hss, hrs, ssx, rsx, ssy, rsy, ssz, rsz
):
    row, grp = lax.axis_index("row"), lax.axis_index("grp")
    others = [lax.rem(grp + k, groups) for k in range(1, groups)]
    order = far_first(n)
    half = n // 2
    side, seat = row // half, lax.rem(row, half)
    near_order = list(range(1, half))
    top = float(jnp.finfo(bf16).max)
    width = acc.shape[0]
    left = layout_of(width)[1]
    pieces = ((0, left), (left, qout.shape[0]))

    def peer(k):
        return side * half + lax.rem(seat + k, half)

    def source(k):
        return lax.rem(seat + half - k, half)

    def across(r):
        plane = n // PLANES
        return n - plane - r + 2 * lax.rem(r, plane)

    mate = across(row)

    def remote(src, dst, ss, rs, where):
        copy = pltpu.make_async_remote_copy(
            src_ref=src, dst_ref=dst, send_sem=ss, recv_sem=rs, device_id=where, device_id_type=MESH
        )
        copy.start()
        return copy

    def share_of(to):
        size, wide = cols.shape[2], cols.shape[3]
        down = pl.ds(pl.multiple_of(grp * size, size), size)
        return tokens.at[down, pl.ds(pl.multiple_of(to * wide, wide), wide)]

    plan = [(k, True) for k in near_order] + [(0, True)] + [(k, False) for k in near_order] + [(0, False)]
    loads = []
    for slot, (k, helping) in enumerate(plan):
        index = across(peer(k)) if helping else peer(k)
        load = pltpu.make_async_copy(grad.at[index], stage.at[slot], lsem.at[slot])
        load.start()
        loads.append((index, load))
    greet(n, groups, others)
    fsends, nsends = {}, {}
    for slot, (k, helping) in enumerate(plan):
        index, load = loads[slot]
        load.wait()
        value = jnp.clip(stage[slot], -top, top).astype(bf16)
        if k == 0:
            (afar if helping else near)[seat] = value
            continue
        raw[slot] = value
        if helping:
            fsends[k] = remote(raw.at[slot], afar.at[seat], fss.at[k], frs.at[k], (grp, peer(k)))
        else:
            nsends[k] = remote(raw.at[slot], near.at[seat], nss.at[k], nrs.at[k], (grp, peer(k)))

    fetch = pltpu.make_async_copy(weight, old, wsem)
    fetch.start()
    names = pltpu.make_async_copy(listed, owner, osem)
    names.start()
    naming = remote(listed, theirs_of, oss, ors, (grp + 1 - 2 * lax.rem(grp, CORES), row))
    acc[...] = dot_t(afar[seat], afar[seat])
    for k in near_order:
        fsends[k].wait_recv()
        acc[...] += dot_t(afar[source(k)], afar[source(k)])
    pack(acc, gout)
    cross = []
    for part_of, (low, high) in enumerate(pieces):
        rows = pl.ds(low, high - low)
        cross.append(remote(gout.at[rows], gin.at[rows], css.at[part_of], crs.at[part_of], (grp, mate)))

    full[...] = dot_t(near[seat], near[seat])
    for k in near_order:
        nsends[k].wait_recv()
        full[...] += dot_t(near[source(k)], near[source(k)])
    tsends = {}
    for k in order:
        to = lax.rem(row + k, n)
        tsends[k] = remote(share_of(to), cols.at[grp, row], tss.at[k], trs.at[k], (grp, to))
    own = pltpu.make_async_copy(share_of(row), cols.at[grp, row], own_sem)
    own.start()

    pack(full, gsum)

    def put_sum(i, j, value):
        acc[block(i), block(j)] = value

    for part_of, (low, high) in enumerate(pieces):
        cross[part_of].wait_recv()
        gsum[low:high] = gsum[low:high] + gin[low:high]
        unpack(gsum, width, put_sum, low, high)

    total = acc[...]
    down, right = iotas(total.shape[0])
    eye = down == right
    norm2 = jnp.sum(jnp.where(eye, total, 0.0), keepdims=True)
    scale = 1.0 / (jnp.sqrt(norm2) + 1e-07)
    gh[...], gl[...] = split(jnp.where(norm2 < jnp.inf, scale * (scale * total), 0.0))

    def whole(high, low):
        return high[...].astype(f32) + low[...].astype(f32)

    for turn in range(ITERS):
        ph[...] = (coef_b * gh[...].astype(f32) + coef_c * dot(gh[...], gh[...])).astype(bf16)
        if turn == 0:
            factor = jnp.where(eye, coef_a, 0.0) + ph[...].astype(f32)
        else:
            factor = coef_a * whole(qh, ql) + (dot(qh[...], ph[...]) + dot(ql[...], ph[...]))
        if turn < ITERS - 1:
            qh[...], ql[...] = split(factor)
            th[...], tl[...] = split(coef_a * whole(gh, gl) + (dot(gh[...], ph[...]) + dot(gl[...], ph[...])))
            gh[...], gl[...] = split(coef_a * whole(th, tl) + (dot_t(ph[...], th[...]) + dot_t(ph[...], tl[...])))
        else:
            factor = scale * factor
            diagonal = jnp.sum(jnp.where(eye, factor, 0.0), axis=0, keepdims=True)
            dout[...] = jnp.broadcast_to(diagonal, dout.shape)
            full[...] = jnp.where(eye, 0.0, factor)
    pack(full, qout)
    outline = remote(dout, din, ess, ers, (grp, mate))
    recross = []
    for part_of, (low, high) in enumerate(pieces):
        rows = pl.ds(low, high - low)
        recross.append(remote(qout.at[rows], qin.at[rows], dss.at[part_of], drs.at[part_of], (grp, mate)))
    qh[...] = full[...].astype(bf16)

    def apply(value, columns, diagonal):
        return (value[:, columns].astype(f32) * diagonal[:1, columns] + dot(value, qh[:, columns])).astype(bf16)

    asends, bsends = {}, {}
    for k in near_order:
        at = lax.rem(seat + k, half)
        near[at] = apply(near[at], slice(None), dout)
        asends[k] = remote(near.at[at], back.at[row], ass.at[k], ars.at[k], (grp, peer(k)))
    back[row] = apply(near[seat], slice(None), dout)

    own.wait()
    for k in order:
        tsends[k].wait_recv()
    gsends = []
    for j, g in enumerate(others):
        gsends.append(remote(cols.at[grp], cols.at[grp], gss.at[j], grs.at[j], (g, row)))

    def put_factor(i, j, value):
        qh[block(i), block(j)] = value.astype(bf16)

    outline.wait_recv()
    for part_of, (low, high) in enumerate(pieces):
        recross[part_of].wait_recv()
        unpack(qin, width, put_factor, low, high)
        columns = slice(part_of * width // 2, (part_of + 1) * width // 2)
        for k in near_order:
            at = lax.rem(seat + k, half)
            update[at, :, columns] = apply(afar[at], columns, din)
            bsends[part_of, k] = remote(
                update.at[at, :, columns], back.at[mate, :, columns],
                bss.at[part_of, k], brs.at[part_of, k], (grp, peer(k))
            )
    back[mate] = apply(afar[seat], slice(None), din)
    fetch.wait()
    names.wait()

    twin = grp + 1 - 2 * lax.rem(grp, CORES)
    first_core = lax.rem(grp, CORES) == 0
    swaps = []

    def renew(slot, index):
        value = (old[index].astype(f32) - step_size * back[index].astype(f32)).astype(bf16)
        fresh[index] = value
        piece = width // groups
        blocks = [value[:, g * piece : (g + 1) * piece] for g in range(groups)]
        halves = [jnp.concatenate(blocks[c::CORES], axis=1) for c in range(CORES)]
        mine[index] = jnp.where(first_core, halves[0], halves[1])
        given[index] = jnp.where(first_core, halves[1], halves[0])
        swaps.append(remote(given.at[index], theirs.at[index], hss.at[slot], hrs.at[slot], (twin, row)))

    renew(0, row)
    for k in near_order:
        asends[k].wait_recv()
        renew(k, side * half + source(k))
    renew(half, mate)
    for copy in gsends:
        copy.wait_recv()
    for k in near_order:
        bsends[0, k].wait_recv()
        bsends[1, k].wait_recv()
        renew(half + k, across(side * half + source(k)))

    naming.wait_recv()
    for copy in swaps:
        copy.wait_recv()
    project(
        n, groups, remote, (owner, theirs_of), counts, (mine, theirs), mixed, cols, got1, gotx, goty, sum2, sum3, gotz,
        ssx, rsx, ssy, rsy, ssz, rsz
    )
    naming.wait_send()
    for copy in swaps:
        copy.wait_send()
    for copy in cross + recross + [outline]:
        copy.wait_send()
    for k in order:
        tsends[k].wait_send()
    for copy in gsends:
        copy.wait_send()
    for k in near_order:
        fsends[k].wait_send()
        nsends[k].wait_send()
        asends[k].wait_send()
        bsends[0, k].wait_send()
        bsends[1, k].wait_send()


def project(
    n, groups, remote, owners, counts, weights, mixed, cols, got1, gotx, goty, sum2, sum3, gotz,
    ssx, rsx, ssy, rsy, ssz, rsz
):
    row, grp = lax.axis_index("row"), lax.axis_index("grp")
    lanes, ys = n // PLANES, groups // CORES
    z, x = row // lanes, lax.rem(row, lanes)
    y, core = grp // CORES, lax.rem(grp, CORES)
    count, piece = mixed.shape
    order = far_first(PLANES) + [0]
    two, three, four = {}, {}, {}

    def matrices_of(owner, b):
        first, last = jnp.int32(n), jnp.int32(-1)
        for e in range(n):
            hit = owner[e] == b
            first = jnp.minimum(first, jnp.where(hit, e, n))
            last = jnp.maximum(last, jnp.where(hit, e, -1))
        return first, last

    def to_x(k, j, src, dst):
        where = (grp, z * lanes + lax.rem(x + j, lanes))
        return remote(src, dst, ssx.at[k, j], rsx.at[k, j], where)

    def to_y(k, j, src, dst):
        where = (lax.rem(y + j, ys) * CORES + core, row)
        return remote(src, dst, ssy.at[k, j], rsy.at[k, j], where)

    def stage1(turn):
        k = order[turn]
        two[k] = []
        for j in range(lanes):
            b = lax.rem(z + k, PLANES) * lanes + lax.rem(x + j, lanes)
            tok = cols[:, b].reshape(count, cols.shape[3])
            total = jnp.zeros((count, ys * piece), f32)
            for owner, weight in zip(owners, weights):
                first, last = matrices_of(owner, b)
                total = total + jnp.where(last >= 0, dot(tok, weight[jnp.minimum(first, n - 1)]), 0.0)
                total = total + jnp.where(last > first, dot(tok, weight[jnp.maximum(last, 0)]), 0.0)
            total = (total * groups ** (-0.5)).astype(bf16)
            for i in range(ys):
                got1[k, j, i] = total[:, i * piece : (i + 1) * piece]
        if turn % 2 == 1:
            for j in range(1, lanes):
                two[k].append(to_x(k, j, got1.at[k, j], gotx.at[k, j]))
        else:
            for i in range(1, ys):
                two[k].append(to_y(k, i, got1.at[k, :, lax.rem(y + i, ys)], goty.at[k, i]))

    def stage3(turn):
        k = order[turn]
        three[k] = []
        for copy in two[k]:
            copy.wait_recv()
        if turn % 2 == 1:
            for i in reversed(range(ys)):
                at = lax.rem(y + i, ys)
                total = got1[k, 0, at].astype(f32)
                for j in range(1, lanes):
                    total = total + gotx[k, j, at].astype(f32)
                sum2[k, i] = total.astype(bf16)
                if i:
                    three[k].append(to_y(k, i, sum2.at[k, i], goty.at[k, i, 0]))
        else:
            for j in reversed(range(lanes)):
                total = got1[k, j, y].astype(f32)
                for i in range(1, ys):
                    total = total + goty[k, i, j].astype(f32)
                sum2[k, j] = total.astype(bf16)
                if j:
                    three[k].append(to_x(k, j, sum2.at[k, j], gotx.at[k, j, 0]))

    def stage4(turn):
        k = order[turn]
        for copy in three[k]:
            copy.wait_recv()
        total = sum2[k, 0].astype(f32)
        if turn % 2 == 1:
            for i in range(1, ys):
                total = total + goty[k, i, 0].astype(f32)
        else:
            for j in range(1, lanes):
                total = total + gotx[k, j, 0].astype(f32)
        if k == 0:
            return total
        sum3[k] = total.astype(bf16)
        four[k] = remote(
            sum3.at[k], gotz.at[k], ssz.at[k], rsz.at[k], (grp, lax.rem(z + k, PLANES) * lanes + x)
        )

    final = None
    for turn in range(PLANES + LAGS[1]):
        if turn < PLANES:
            stage1(turn)
        for stage, lag in zip((stage3, stage4), LAGS):
            if lag <= turn < PLANES + lag:
                final = stage(turn - lag)
    for k in order[:-1]:
        four[k].wait_recv()
        final = final + gotz[k].astype(f32)
    live = lax.broadcasted_iota(jnp.int32, (count, piece), 0) < counts[0]
    mixed[...] = jnp.where(live, final, 0.0).astype(bf16)
    for k in order:
        for copy in two[k] + three[k]:
            copy.wait_send()
        if k:
            four[k].wait_send()


def store_kernel(fresh, mixed, new_weight, out, fsem, msem):
    copies = [pltpu.make_async_copy(mixed, out, msem)]
    for i in range(fresh.shape[0]):
        copies.append(pltpu.make_async_copy(fresh.at[i], new_weight.at[i], fsem.at[i]))
    for copy in copies:
        copy.start()
    for copy in copies:
        copy.wait()


VM = pl.BlockSpec(memory_space=pltpu.VMEM)
SM = pl.BlockSpec(memory_space=pltpu.SMEM)
HBM = pl.BlockSpec(memory_space=pltpu.HBM)


def body(grad, weight, owner, tokens, counts):
    ranks = lax.axis_size("row")
    groups = lax.axis_size("grp")
    number, rows, width = grad.shape
    assert number == ranks
    half = ranks // 2
    lanes, ys = ranks // PLANES, groups // CORES
    count = tokens.shape[0]
    share, piece = count // groups, width // groups
    dma = pltpu.SemaphoreType.DMA
    vmem = pltpu.VMEM
    packed = vmem((packed_rows(width), TILE), f32)
    buffers = [
        vmem((groups, ranks, share, rows), bf16),
        vmem((ranks, rows, width), bf16),
        vmem((ranks, rows, width), bf16),
        vmem((ranks, rows, width), f32),
        vmem((ranks, rows, width), bf16),
        vmem((half, rows, width), bf16),
        vmem((half, rows, width), bf16),
        vmem((half, rows, width), bf16),
    ]
    buffers += [vmem((width, width), f32)] * 2
    buffers += [packed] * 3
    buffers += [vmem((packed_rows(width), TILE), bf16)] * 2
    buffers += [vmem((8, width), f32)] * 2
    buffers += [vmem((width, width), bf16)] * 7
    buffers += [vmem((ranks, rows, width // CORES), bf16)] * 3
    buffers += [
        vmem((PLANES, lanes, ys, count, piece), bf16),
        vmem((PLANES, lanes, ys, count, piece), bf16),
        vmem((PLANES, ys, lanes, count, piece), bf16),
        vmem((PLANES, max(ys, lanes), count, piece), bf16),
        vmem((PLANES, count, piece), bf16),
        vmem((PLANES, count, piece), bf16),
    ]
    semaphores = [dma((ranks,))]
    semaphores += [dma((half,))] * 4
    semaphores += [dma((2,))] * 4
    semaphores += [dma((half,))] * 2
    semaphores += [dma((2, half))] * 2
    semaphores += [dma((ranks,))] * 2
    semaphores += [dma((groups,))] * 2
    semaphores += [dma] * 2
    semaphores += [pltpu.SMEM((number,), jnp.int32), dma]
    semaphores += [dma] * 2
    semaphores += [pltpu.SMEM((number,), jnp.int32), dma, dma]
    semaphores += [dma((ranks,))] * 2
    semaphores += [dma((PLANES, lanes))] * 2
    semaphores += [dma((PLANES, ys))] * 2
    semaphores += [dma((PLANES,))] * 2
    lane = 128
    held = sum(
        math.prod(b.shape[:-1]) * pl.cdiv(b.shape[-1], lane) * lane * jnp.dtype(b.dtype).itemsize for b in buffers
    )
    fresh, mixed = pl.pallas_call(
        functools.partial(step_kernel, ranks, groups),
        out_shape=[
            jax.ShapeDtypeStruct((ranks, rows, width), bf16),
            jax.ShapeDtypeStruct((count, piece), bf16),
        ],
        in_specs=[SM, HBM, HBM, HBM, HBM],
        out_specs=[VM, VM],
        scratch_shapes=buffers + semaphores,
        compiler_params=pltpu.CompilerParams(
            collective_id=0, has_side_effects=True, vmem_limit_bytes=held + SPARE
        ),
        name="step",
    )(counts, *[pltpu.with_memory_space_constraint(a, pltpu.HBM) for a in (owner[:, 0], grad, weight, tokens)])
    return pl.pallas_call(
        store_kernel,
        out_shape=[jax.ShapeDtypeStruct(a.shape, bf16) for a in (fresh, mixed)],
        in_specs=[VM, VM],
        out_specs=[HBM, HBM],
        scratch_shapes=[dma((ranks,)), dma],
        compiler_params=pltpu.CompilerParams(vmem_limit_bytes=SPARE),
        name="store",
    )(fresh, mixed)


def solution(mesh):
    placed = (
        P("grp", "row", None),
        P("grp", "row", None),
        P("grp", None),
        P("row", None),
        P("row"),
    )
    return jax.shard_map(
        body,
        mesh=mesh,
        in_specs=placed,
        out_specs=(P("grp", "row", None), P("row", "grp")),
        check_vma=False,
    )
```

```python
import functools
import math

import jax
import jax.numpy as jnp
from jax import lax
from jax.experimental import pallas as pl
from jax.experimental.pallas import tpu as pltpu
from jax.sharding import PartitionSpec as P

ITERS = 5
CORES = 2
LAGS = (2, 4)
TILE = 128
PAD = 16
PLANES = 4
SPARE = 3 * 1024 * 1024

coef_a = 3.4445
coef_b = -4.775
coef_c = 2.0315
step_size = 0.5

f32 = jnp.float32
bf16 = jnp.bfloat16
MESH = pl.DeviceIdType.MESH


def far_first(n):
    return sorted(range(1, n), key=lambda k: abs(k - n // 2))


def greet(n, groups, grp_shifts):
    row, grp = lax.axis_index("row"), lax.axis_index("grp")
    barrier = pltpu.get_barrier_semaphore()
    for k in range(1, n):
        pl.semaphore_signal(
            barrier, inc=1, device_id=(grp, lax.rem(row + k, n)), device_id_type=MESH
        )
    for g in grp_shifts:
        pl.semaphore_signal(barrier, inc=1, device_id=(g, row), device_id_type=MESH)
    pl.semaphore_wait(barrier, n - 1 + len(grp_shifts))


def split(v):
    high = v.astype(bf16)
    return high, (v - high.astype(f32)).astype(bf16)


def dot(a, b):
    return jnp.dot(a, b, preferred_element_type=f32)


def dot_t(a, b):
    return lax.dot_general(a, b, (((0,), (0,)), ((), ())), preferred_element_type=f32)


def iotas(size):
    shape = (size, size)
    return lax.broadcasted_iota(jnp.int32, shape, 0), lax.broadcasted_iota(jnp.int32, shape, 1)


def block(i):
    return slice(i * TILE, (i + 1) * TILE)


def packed_rows(width):
    count = width // TILE
    return (count * (count - 1) // 2 + count // 2) * TILE + count // 2 * PAD


def layout_of(width):
    count = width // TILE
    middle = count // 2
    items, at, left = [], 0, 0
    for low, high in ((0, middle), (middle, count)):
        for i in range(low, high):
            for j in range(i + 1, count):
                items.append((at, i, j))
                at += TILE
        for i in range(low, high, 2):
            items.append((at, i, i))
            at += TILE + PAD
        left = left or at
    return items, left


def pack(full, out):
    row, col = iotas(TILE)
    for at, i, j in layout_of(full.shape[0])[0]:
        if i < j:
            out[at : at + TILE] = full[block(i), block(j)].astype(out.dtype)
            continue
        one, two = full[block(i), block(i)], full[block(i + 1), block(i + 1)]
        out[at : at + TILE] = jnp.where(row <= col, one, two).astype(out.dtype)
        diagonal = jnp.sum(jnp.where(row == col, two, 0.0), axis=0, keepdims=True)
        out[at + TILE : at + TILE + PAD] = jnp.broadcast_to(diagonal, (PAD, TILE)).astype(out.dtype)


def unpack(packed, width, put, low, high):
    row, col = iotas(TILE)
    for at, i, j in layout_of(width)[0]:
        if not low <= at < high:
            continue
        value = packed[at : at + TILE].astype(f32)
        turned = value.T
        if i < j:
            put(i, j, value)
            put(j, i, turned)
            continue
        diagonal = jnp.broadcast_to(packed[at + TILE : at + TILE + PAD].astype(f32)[:1], (TILE, TILE))
        put(i, i, jnp.where(row <= col, value, turned))
        put(i + 1, i + 1, jnp.where(row > col, value, jnp.where(row < col, turned, diagonal)))


def step_kernel(
    n, groups, counts, listed, grad, weight, tokens, fresh, mixed, cols, back, old,
    stage, raw, afar, near, update, acc, full, gout, gin, gsum, qout, qin, dout, din, gh, gl, ph, qh, ql, th, tl,
    mine, theirs, given, got1, gotx, goty, sum2, sum3, gotz,
    lsem, fss, frs, nss, nrs, css, crs, dss, drs, ass, ars, bss, brs, tss, trs, gss, grs, own_sem, wsem, owner, osem, ess, ers,
    theirs_of, oss, ors, hss, hrs, ssx, rsx, ssy, rsy, ssz, rsz
):
    row, grp = lax.axis_index("row"), lax.axis_index("grp")
    others = [lax.rem(grp + k, groups) for k in range(1, groups)]
    order = far_first(n)
    half = n // 2
    side, seat = row // half, lax.rem(row, half)
    near_order = list(range(1, half))
    top = float(jnp.finfo(bf16).max)
    width = acc.shape[0]
    left = layout_of(width)[1]
    pieces = ((0, left), (left, qout.shape[0]))

    def peer(k):
        return side * half + lax.rem(seat + k, half)

    def source(k):
        return lax.rem(seat + half - k, half)

    def across(r):
        plane = n // PLANES
        return n - plane - r + 2 * lax.rem(r, plane)

    mate = across(row)

    def remote(src, dst, ss, rs, where):
        copy = pltpu.make_async_remote_copy(
            src_ref=src, dst_ref=dst, send_sem=ss, recv_sem=rs, device_id=where, device_id_type=MESH
        )
        copy.start()
        return copy

    def share_of(to):
        size, wide = cols.shape[2], cols.shape[3]
        down = pl.ds(pl.multiple_of(grp * size, size), size)
        return tokens.at[down, pl.ds(pl.multiple_of(to * wide, wide), wide)]

    plan = [(k, True) for k in near_order] + [(0, True)] + [(k, False) for k in near_order] + [(0, False)]
    loads = []
    for slot, (k, helping) in enumerate(plan):
        index = across(peer(k)) if helping else peer(k)
        load = pltpu.make_async_copy(grad.at[index], stage.at[slot], lsem.at[slot])
        load.start()
        loads.append((index, load))
    greet(n, groups, others)
    fsends, nsends = {}, {}
    for slot, (k, helping) in enumerate(plan):
        index, load = loads[slot]
        load.wait()
        value = jnp.clip(stage[slot], -top, top).astype(bf16)
        if k == 0:
            (afar if helping else near)[seat] = value
            continue
        raw[slot] = value
        if helping:
            fsends[k] = remote(raw.at[slot], afar.at[seat], fss.at[k], frs.at[k], (grp, peer(k)))
        else:
            nsends[k] = remote(raw.at[slot], near.at[seat], nss.at[k], nrs.at[k], (grp, peer(k)))

    fetch = pltpu.make_async_copy(weight, old, wsem)
    fetch.start()
    names = pltpu.make_async_copy(listed, owner, osem)
    names.start()
    naming = remote(listed, theirs_of, oss, ors, (grp + 1 - 2 * lax.rem(grp, CORES), row))
    acc[...] = dot_t(afar[seat], afar[seat])
    for k in near_order:
        fsends[k].wait_recv()
        acc[...] += dot_t(afar[source(k)], afar[source(k)])
    pack(acc, gout)
    cross = []
    for part_of, (low, high) in enumerate(pieces):
        rows = pl.ds(low, high - low)
        cross.append(remote(gout.at[rows], gin.at[rows], css.at[part_of], crs.at[part_of], (grp, mate)))

    full[...] = dot_t(near[seat], near[seat])
    for k in near_order:
        nsends[k].wait_recv()
        full[...] += dot_t(near[source(k)], near[source(k)])
    tsends = {}
    for k in order:
        to = lax.rem(row + k, n)
        tsends[k] = remote(share_of(to), cols.at[grp, row], tss.at[k], trs.at[k], (grp, to))
    own = pltpu.make_async_copy(share_of(row), cols.at[grp, row], own_sem)
    own.start()

    pack(full, gsum)

    def put_sum(i, j, value):
        acc[block(i), block(j)] = value

    for part_of, (low, high) in enumerate(pieces):
        cross[part_of].wait_recv()
        gsum[low:high] = gsum[low:high] + gin[low:high]
        unpack(gsum, width, put_sum, low, high)

    total = acc[...]
    down, right = iotas(total.shape[0])
    eye = down == right
    norm2 = jnp.sum(jnp.where(eye, total, 0.0), keepdims=True)
    scale = 1.0 / (jnp.sqrt(norm2) + 1e-07)
    gh[...], gl[...] = split(jnp.where(norm2 < jnp.inf, scale * (scale * total), 0.0))

    def whole(high, low):
        return high[...].astype(f32) + low[...].astype(f32)

    for turn in range(ITERS):
        ph[...] = (coef_b * gh[...].astype(f32) + coef_c * dot(gh[...], gh[...])).astype(bf16)
        if turn == 0:
            factor = jnp.where(eye, coef_a, 0.0) + ph[...].astype(f32)
        else:
            factor = coef_a * whole(qh, ql) + (dot(qh[...], ph[...]) + dot(ql[...], ph[...]))
        if turn < ITERS - 1:
            qh[...], ql[...] = split(factor)
            th[...], tl[...] = split(coef_a * whole(gh, gl) + (dot(gh[...], ph[...]) + dot(gl[...], ph[...])))
            gh[...], gl[...] = split(coef_a * whole(th, tl) + (dot_t(ph[...], th[...]) + dot_t(ph[...], tl[...])))
        else:
            factor = scale * factor
            diagonal = jnp.sum(jnp.where(eye, factor, 0.0), axis=0, keepdims=True)
            dout[...] = jnp.broadcast_to(diagonal, dout.shape)
            full[...] = jnp.where(eye, 0.0, factor)
    pack(full, qout)
    outline = remote(dout, din, ess, ers, (grp, mate))
    recross = []
    for part_of, (low, high) in enumerate(pieces):
        rows = pl.ds(low, high - low)
        recross.append(remote(qout.at[rows], qin.at[rows], dss.at[part_of], drs.at[part_of], (grp, mate)))
    qh[...] = full[...].astype(bf16)

    def apply(value, columns, diagonal):
        return (value[:, columns].astype(f32) * diagonal[:1, columns] + dot(value, qh[:, columns])).astype(bf16)

    asends, bsends = {}, {}
    for k in near_order:
        at = lax.rem(seat + k, half)
        near[at] = apply(near[at], slice(None), dout)
        asends[k] = remote(near.at[at], back.at[row], ass.at[k], ars.at[k], (grp, peer(k)))
    back[row] = apply(near[seat], slice(None), dout)

    own.wait()
    for k in order:
        tsends[k].wait_recv()
    gsends = []
    for j, g in enumerate(others):
        gsends.append(remote(cols.at[grp], cols.at[grp], gss.at[j], grs.at[j], (g, row)))

    def put_factor(i, j, value):
        qh[block(i), block(j)] = value.astype(bf16)

    outline.wait_recv()
    for part_of, (low, high) in enumerate(pieces):
        recross[part_of].wait_recv()
        unpack(qin, width, put_factor, low, high)
        columns = slice(part_of * width // 2, (part_of + 1) * width // 2)
        for k in near_order:
            at = lax.rem(seat + k, half)
            update[at, :, columns] = apply(afar[at], columns, din)
            bsends[part_of, k] = remote(
                update.at[at, :, columns], back.at[mate, :, columns],
                bss.at[part_of, k], brs.at[part_of, k], (grp, peer(k))
            )
    back[mate] = apply(afar[seat], slice(None), din)
    fetch.wait()
    names.wait()

    twin = grp + 1 - 2 * lax.rem(grp, CORES)
    first_core = lax.rem(grp, CORES) == 0
    swaps = []

    def renew(slot, index):
        value = (old[index].astype(f32) - step_size * back[index].astype(f32)).astype(bf16)
        fresh[index] = value
        piece = width // groups
        blocks = [value[:, g * piece : (g + 1) * piece] for g in range(groups)]
        halves = [jnp.concatenate(blocks[c::CORES], axis=1) for c in range(CORES)]
        mine[index] = jnp.where(first_core, halves[0], halves[1])
        given[index] = jnp.where(first_core, halves[1], halves[0])
        swaps.append(remote(given.at[index], theirs.at[index], hss.at[slot], hrs.at[slot], (twin, row)))

    renew(0, row)
    for k in near_order:
        asends[k].wait_recv()
        renew(k, side * half + source(k))
    renew(half, mate)
    for copy in gsends:
        copy.wait_recv()
    for k in near_order:
        bsends[0, k].wait_recv()
        bsends[1, k].wait_recv()
        renew(half + k, across(side * half + source(k)))

    project(
        n, groups, remote, [naming] + swaps, (owner, theirs_of), counts, (mine, theirs), mixed, cols, got1, gotx, goty, sum2, sum3, gotz,
        ssx, rsx, ssy, rsy, ssz, rsz
    )
    naming.wait_send()
    for copy in swaps:
        copy.wait_send()
    for copy in cross + recross + [outline]:
        copy.wait_send()
    for k in order:
        tsends[k].wait_send()
    for copy in gsends:
        copy.wait_send()
    for k in near_order:
        fsends[k].wait_send()
        nsends[k].wait_send()
        asends[k].wait_send()
        bsends[0, k].wait_send()
        bsends[1, k].wait_send()


def project(
    n, groups, remote, arrivals, owners, counts, weights, mixed, cols, got1, gotx, goty, sum2, sum3, gotz,
    ssx, rsx, ssy, rsy, ssz, rsz
):
    row, grp = lax.axis_index("row"), lax.axis_index("grp")
    lanes, ys = n // PLANES, groups // CORES
    z, x = row // lanes, lax.rem(row, lanes)
    y, core = grp // CORES, lax.rem(grp, CORES)
    count, piece = mixed.shape
    order = far_first(PLANES) + [0]
    two, three, four = {}, {}, {}

    def matrices_of(owner, b):
        first, last = jnp.int32(n), jnp.int32(-1)
        for e in range(n):
            hit = owner[e] == b
            first = jnp.minimum(first, jnp.where(hit, e, n))
            last = jnp.maximum(last, jnp.where(hit, e, -1))
        return first, last

    def to_x(k, j, src, dst):
        where = (grp, z * lanes + lax.rem(x + j, lanes))
        return remote(src, dst, ssx.at[k, j], rsx.at[k, j], where)

    def to_y(k, j, src, dst):
        where = (lax.rem(y + j, ys) * CORES + core, row)
        return remote(src, dst, ssy.at[k, j], rsy.at[k, j], where)

    def stage1(turn):
        k = order[turn]
        two[k] = []
        totals = [jnp.zeros((count, ys * piece), f32)] * lanes
        for source, (owner, weight) in enumerate(zip(owners, weights)):
            if turn == 0 and source == 1:
                for copy in arrivals:
                    copy.wait_recv()
            for j in range(lanes):
                b = lax.rem(z + k, PLANES) * lanes + lax.rem(x + j, lanes)
                tok = cols[:, b].reshape(count, cols.shape[3])
                first, last = matrices_of(owner, b)
                totals[j] = totals[j] + jnp.where(last >= 0, dot(tok, weight[jnp.minimum(first, n - 1)]), 0.0)
                totals[j] = totals[j] + jnp.where(last > first, dot(tok, weight[jnp.maximum(last, 0)]), 0.0)
        for j, total in enumerate(totals):
            total = (total * groups ** (-0.5)).astype(bf16)
            for i in range(ys):
                got1[k, j, i] = total[:, i * piece : (i + 1) * piece]
        if turn % 2 == 1:
            for j in range(1, lanes):
                two[k].append(to_x(k, j, got1.at[k, j], gotx.at[k, j]))
        else:
            for i in range(1, ys):
                two[k].append(to_y(k, i, got1.at[k, :, lax.rem(y + i, ys)], goty.at[k, i]))

    def stage3(turn):
        k = order[turn]
        three[k] = []
        for copy in two[k]:
            copy.wait_recv()
        if turn % 2 == 1:
            for i in reversed(range(ys)):
                at = lax.rem(y + i, ys)
                total = got1[k, 0, at].astype(f32)
                for j in range(1, lanes):
                    total = total + gotx[k, j, at].astype(f32)
                sum2[k, i] = total.astype(bf16)
                if i:
                    three[k].append(to_y(k, i, sum2.at[k, i], goty.at[k, i, 0]))
        else:
            for j in reversed(range(lanes)):
                total = got1[k, j, y].astype(f32)
                for i in range(1, ys):
                    total = total + goty[k, i, j].astype(f32)
                sum2[k, j] = total.astype(bf16)
                if j:
                    three[k].append(to_x(k, j, sum2.at[k, j], gotx.at[k, j, 0]))

    def stage4(turn):
        k = order[turn]
        for copy in three[k]:
            copy.wait_recv()
        total = sum2[k, 0].astype(f32)
        if turn % 2 == 1:
            for i in range(1, ys):
                total = total + goty[k, i, 0].astype(f32)
        else:
            for j in range(1, lanes):
                total = total + gotx[k, j, 0].astype(f32)
        if k == 0:
            return total
        sum3[k] = total.astype(bf16)
        four[k] = remote(
            sum3.at[k], gotz.at[k], ssz.at[k], rsz.at[k], (grp, lax.rem(z + k, PLANES) * lanes + x)
        )

    final = None
    for turn in range(PLANES + LAGS[1]):
        if turn < PLANES:
            stage1(turn)
        for stage, lag in zip((stage3, stage4), LAGS):
            if lag <= turn < PLANES + lag:
                final = stage(turn - lag)
    for k in order[:-1]:
        four[k].wait_recv()
        final = final + gotz[k].astype(f32)
    live = lax.broadcasted_iota(jnp.int32, (count, piece), 0) < counts[0]
    mixed[...] = jnp.where(live, final, 0.0).astype(bf16)
    for k in order:
        for copy in two[k] + three[k]:
            copy.wait_send()
        if k:
            four[k].wait_send()


def store_kernel(fresh, mixed, new_weight, out, fsem, msem):
    copies = [pltpu.make_async_copy(mixed, out, msem)]
    for i in range(fresh.shape[0]):
        copies.append(pltpu.make_async_copy(fresh.at[i], new_weight.at[i], fsem.at[i]))
    for copy in copies:
        copy.start()
    for copy in copies:
        copy.wait()


VM = pl.BlockSpec(memory_space=pltpu.VMEM)
SM = pl.BlockSpec(memory_space=pltpu.SMEM)
HBM = pl.BlockSpec(memory_space=pltpu.HBM)


def body(grad, weight, owner, tokens, counts):
    ranks = lax.axis_size("row")
    groups = lax.axis_size("grp")
    number, rows, width = grad.shape
    assert number == ranks
    half = ranks // 2
    lanes, ys = ranks // PLANES, groups // CORES
    count = tokens.shape[0]
    share, piece = count // groups, width // groups
    dma = pltpu.SemaphoreType.DMA
    vmem = pltpu.VMEM
    packed = vmem((packed_rows(width), TILE), f32)
    buffers = [
        vmem((groups, ranks, share, rows), bf16),
        vmem((ranks, rows, width), bf16),
        vmem((ranks, rows, width), bf16),
        vmem((ranks, rows, width), f32),
        vmem((ranks, rows, width), bf16),
        vmem((half, rows, width), bf16),
        vmem((half, rows, width), bf16),
        vmem((half, rows, width), bf16),
    ]
    buffers += [vmem((width, width), f32)] * 2
    buffers += [packed] * 3
    buffers += [vmem((packed_rows(width), TILE), bf16)] * 2
    buffers += [vmem((8, width), f32)] * 2
    buffers += [vmem((width, width), bf16)] * 7
    buffers += [vmem((ranks, rows, width // CORES), bf16)] * 3
    buffers += [
        vmem((PLANES, lanes, ys, count, piece), bf16),
        vmem((PLANES, lanes, ys, count, piece), bf16),
        vmem((PLANES, ys, lanes, count, piece), bf16),
        vmem((PLANES, max(ys, lanes), count, piece), bf16),
        vmem((PLANES, count, piece), bf16),
        vmem((PLANES, count, piece), bf16),
    ]
    semaphores = [dma((ranks,))]
    semaphores += [dma((half,))] * 4
    semaphores += [dma((2,))] * 4
    semaphores += [dma((half,))] * 2
    semaphores += [dma((2, half))] * 2
    semaphores += [dma((ranks,))] * 2
    semaphores += [dma((groups,))] * 2
    semaphores += [dma] * 2
    semaphores += [pltpu.SMEM((number,), jnp.int32), dma]
    semaphores += [dma] * 2
    semaphores += [pltpu.SMEM((number,), jnp.int32), dma, dma]
    semaphores += [dma((ranks,))] * 2
    semaphores += [dma((PLANES, lanes))] * 2
    semaphores += [dma((PLANES, ys))] * 2
    semaphores += [dma((PLANES,))] * 2
    lane = 128
    held = sum(
        math.prod(b.shape[:-1]) * pl.cdiv(b.shape[-1], lane) * lane * jnp.dtype(b.dtype).itemsize for b in buffers
    )
    fresh, mixed = pl.pallas_call(
        functools.partial(step_kernel, ranks, groups),
        out_shape=[
            jax.ShapeDtypeStruct((ranks, rows, width), bf16),
            jax.ShapeDtypeStruct((count, piece), bf16),
        ],
        in_specs=[SM, HBM, HBM, HBM, HBM],
        out_specs=[VM, VM],
        scratch_shapes=buffers + semaphores,
        compiler_params=pltpu.CompilerParams(
            collective_id=0, has_side_effects=True, vmem_limit_bytes=held + SPARE
        ),
        name="step",
    )(counts, *[pltpu.with_memory_space_constraint(a, pltpu.HBM) for a in (owner[:, 0], grad, weight, tokens)])
    return pl.pallas_call(
        store_kernel,
        out_shape=[jax.ShapeDtypeStruct(a.shape, bf16) for a in (fresh, mixed)],
        in_specs=[VM, VM],
        out_specs=[HBM, HBM],
        scratch_shapes=[dma((ranks,)), dma],
        compiler_params=pltpu.CompilerParams(vmem_limit_bytes=SPARE),
        name="store",
    )(fresh, mixed)


def solution(mesh):
    placed = (
        P("grp", "row", None),
        P("grp", "row", None),
        P("grp", None),
        P("row", None),
        P("row"),
    )
    return jax.shard_map(
        body,
        mesh=mesh,
        in_specs=placed,
        out_specs=(P("grp", "row", None), P("row", "grp")),
        check_vma=False,
    )
```
